32 devices in a mesh: gx: 8 (over y, x, core), gy: 4 (over z).
Axes of the slice: x: 2, y: 2, z: 4, core: 2. Of those that a mesh axis runs over, the one named last changes fastest.
Arguments:
- block_input: bfloat16 [25088, 512], P(('gx', 'gy')), may hold values from -6 to 6
- cotangent: bfloat16 [25088, 512], P(('gx', 'gy')), may hold values from -6 to 6
- live_images: int32 [8], P('gx'), may hold values from 1 to 16, 96 in all
- ln1_gain: bfloat16 [512], replicated, may hold values from 0.25 to 1.75
- ln1_bias: bfloat16 [512], replicated, may hold values from -3 to 3
- qkv_weight: bfloat16 [512, 3, 512], P('gx', None, 'gy'), may hold values from -0.25 to 0.25
- qv_bias: bfloat16 [2, 512], P(None, 'gy'), may hold values from -3 to 3
- rel_table: bfloat16 [169, 16], P(None, 'gy'), may hold values from -4 to 254
- proj_weight: bfloat16 [512, 512], P('gy', 'gx'), may hold values from -0.75 to 0.75
- proj_bias: bfloat16 [512], replicated, may hold values from -3 to 3
- ln2_gain: bfloat16 [512], replicated, may hold values from 0.25 to 1.75
- ln2_bias: bfloat16 [512], replicated, may hold values from -3 to 3
- fc1_weight: bfloat16 [512, 2048], P('gx', 'gy'), may hold values from -0.25 to 0.25
- fc1_bias: bfloat16 [2048], P('gy'), may hold values from -3 to 3
- fc2_weight: bfloat16 [2048, 512], P('gy', 'gx'), may hold values from -0.1875 to 0.1875
- fc2_bias: bfloat16 [512], replicated, may hold values from -3 to 3
Outputs:
- output: bfloat16 [25088, 512], P(('gx', 'gy'))
- d_input: bfloat16 [25088, 512], P(('gx', 'gy'))
- d_ln1_gain: float32 [512], replicated
- d_ln1_bias: float32 [512], replicated
- d_qkv_weight: float32 [512, 3, 512], P('gx', None, 'gy')
- d_qv_bias: float32 [2, 512], P(None, 'gy')
- d_rel_table: float32 [169, 16], P(None, 'gy')
- d_proj_weight: float32 [512, 512], P('gy', 'gx')
- d_proj_bias: float32 [512], replicated
- d_ln2_gain: float32 [512], replicated
- d_ln2_bias: float32 [512], replicated
- d_fc1_weight: float32 [512, 2048], P('gx', 'gy')
- d_fc1_bias: float32 [2048], P('gy')
- d_fc2_weight: float32 [2048, 512], P('gy', 'gx')
- d_fc2_bias: float32 [512], replicated
The draws below stay inside these ranges and needn't reach their ends.
Inputs may be any that keep to these rules, and one draw needn't show every extreme that they name: Image slot s of index i of gx (slots 0 to 15 in order) holds an image exactly when s < live_images[i]; the counts add up to 96.
All inputs are finite; a program needn't handle non-finite values. No bound on the sum of `live_images` on one device may be relied on, other than what follows from the above.
Results may differ from the reference program's by a relative error of at most 0.014.
Values may be sent and summed in bfloat16 or wider, within the bound.
A program may use at most 192 MiB of HBM per device.

```python
import math
import jax
import jax.numpy as jnp
import numpy as np
from jax import lax

C = 512
H = 16
HD = 32
FF = 2048
GRID = 14
WIN = 7
SHIFT = 3
IMG_DEV = 16
TOKENS = 25088
LIVE = 96
RELS = 169
N_GX = 8


def draw_rel_table(key, part):
    key_base = jax.random.fold_in(key, 0)
    drawn = jnp.clip(jax.random.normal(key_base, (RELS, H), jnp.float32), -3.5, 3.5)
    return drawn.astype(jnp.bfloat16)


def shard_levels(own_key, dims, pieces, low, largest):
    def one(position, shards_of):
        draws = jax.random.uniform(jax.random.fold_in(jax.random.fold_in(own_key, 6), position), (shards_of,), jnp.float32, low / len(pieces), largest / len(pieces))
        return jnp.repeat(jnp.exp(draws), dims[position] // shards_of).reshape((-1,) + (1,) * (len(dims) - position - 1))

    loudness = one(*pieces[0])
    for cut in pieces[1:]:
        loudness = loudness * one(*cut)
    return loudness


def profile(count, total, most, skew):
    loads = [(1 << 20) // math.isqrt(rank ** skew) + 1 for rank in range(2, count + 1)]
    rest, holding = total - most - (count - 1), [1] * (count - 1)
    while rest > 0:
        free = [i for i in range(count - 1) if holding[i] < most]
        mass, left = sum([loads[i] for i in free]), rest
        for i in free:
            addition = min(most - holding[i], max(1, left * loads[i] // mass), rest)
            holding[i] = holding[i] + addition
            rest = rest - addition
    return np.array([most] + holding)


def uneven_parts(stream_key, count, total, bound, lean):
    if count == 2:
        one = jax.random.randint(stream_key, (), max(1, total - bound), min(bound, total - 1) + 1)
        return jnp.stack([one, total - one])
    sizes = jnp.asarray(profile(count, total, bound, lean), jnp.int32)
    pairs = (count - 1) // 2
    giver, taker = sizes[1:1 + 2 * pairs:2], sizes[2:2 + 2 * pairs:2]
    slack = jnp.minimum(giver - 1, bound - taker)
    moved = jax.random.randint(jax.random.fold_in(stream_key, 1), (pairs,), 0, 1 << 20) % (slack + 1)
    sizes = sizes.at[1:1 + 2 * pairs:2].set(giver - moved).at[2:2 + 2 * pairs:2].set(taker + moved)
    return sizes[jax.random.permutation(jax.random.fold_in(stream_key, 2), count)]


def noise(rng, dims, width, bound, cuts=(), kind=jnp.bfloat16):
    result = jax.random.normal(rng, dims, jnp.float32) * width
    if len(cuts) > 0:
        result = shard_levels(rng, dims, cuts, -0.22, 0.18) * result
    return jnp.clip(result, min=-bound, max=bound).astype(kind)


def setup_inputs(seed: int = 0) -> dict:
    key_list = jax.random.split(jax.random.key(seed), 17)
    return {
        "block_input": noise(key_list[0], (TOKENS, C), 1.0, 6.0, ((0, 32),)),
        "cotangent": noise(key_list[1], (TOKENS, C), 1.0, 6.0, ((0, 32),)),
        "live_images": uneven_parts(key_list[2], N_GX, LIVE, IMG_DEV, 1).astype(jnp.int32),
        "ln1_gain": jnp.clip(1.0 + 0.15 * jax.random.normal(key_list[3], (C,), jnp.float32), 0.25, 1.75).astype(jnp.bfloat16),
        "ln1_bias": noise(key_list[4], (C,), 0.5, 3.0),
        "qkv_weight": noise(key_list[5], (C, 3, C), C ** -0.5, 0.25, ((0, 8), (2, 4))),
        "qv_bias": noise(key_list[6], (2, C), 0.5, 3.0, ((1, 4),)),
        "rel_table": draw_rel_table(jax.random.fold_in(key_list[16], 71), 0),
        "proj_weight": noise(key_list[8], (C, C), (C // 7) ** -0.5, 0.75, ((0, 4), (1, 8))),
        "proj_bias": noise(key_list[9], (C,), 0.5, 3.0),
        "ln2_gain": jnp.clip(1.0 + 0.15 * jax.random.normal(key_list[10], (C,), jnp.float32), 0.25, 1.75).astype(jnp.bfloat16),
        "ln2_bias": noise(key_list[11], (C,), 0.5, 3.0),
        "fc1_weight": noise(key_list[12], (C, FF), C ** -0.5, 0.25, ((0, 8), (1, 4))),
        "fc1_bias": noise(key_list[13], (FF,), 0.5, 3.0, ((0, 4),)),
        "fc2_weight": noise(key_list[14], (FF, C), (FF // 2) ** -0.5, 0.1875, ((0, 4), (1, 8))),
        "fc2_bias": noise(key_list[15], (C,), 0.5, 3.0),
    }


eps_norm = 1e-05
mask_value = -100.0
inv_root_two = 0.7071067811865476
inv_root_two_pi = 0.3989422804014327

def window_tables():
    win_area = WIN * WIN
    places = jnp.arange(win_area, dtype=jnp.int32)
    in_row = places // WIN
    in_col = places % WIN
    rel_index = (in_row[:, None] - in_row[None, :] + WIN - 1) * (2 * WIN - 1) + (in_col[:, None] - in_col[None, :] + WIN - 1)
    onehot = (rel_index[:, :, None] == jnp.arange(RELS, dtype=jnp.int32)[None, None, :]).astype(jnp.float32)
    win_count = GRID // WIN
    cells = jnp.arange(GRID, dtype=jnp.int32)
    region = jnp.where(cells < GRID - WIN, 0, jnp.where(cells < GRID - SHIFT, 1, 2))
    cell_id = region[:, None] * 3 + region[None, :]
    win_id = cell_id.reshape(win_count, WIN, win_count, WIN).transpose(0, 2, 1, 3).reshape(win_count, win_count, win_area)
    shift_mask = jnp.where(win_id[:, :, :, None] == win_id[:, :, None, :], 0.0, mask_value).astype(jnp.float32)
    return (onehot, shift_mask)

def to_windows(values, head_count):
    image_count = values.shape[0] // (GRID * GRID)
    win_count = GRID // WIN
    cells = values.reshape(image_count, GRID, GRID, head_count, HD)
    cells = jnp.roll(cells, (-SHIFT, -SHIFT), axis=(1, 2))
    cells = cells.reshape(image_count, win_count, WIN, win_count, WIN, head_count, HD)
    return cells.transpose(0, 1, 3, 5, 2, 4, 6).reshape(image_count, win_count, win_count, head_count, WIN * WIN, HD)

def from_windows(windows):
    image_count, win_count, win_other, head_count = windows.shape[:4]
    cells = windows.reshape(image_count, win_count, win_other, head_count, WIN, WIN, HD).transpose(0, 1, 4, 2, 5, 3, 6)
    cells = cells.reshape(image_count, GRID, GRID, head_count, HD)
    cells = jnp.roll(cells, (SHIFT, SHIFT), axis=(1, 2))
    return cells.reshape(image_count * GRID * GRID, head_count * HD)

def as_float(values):
    return values.astype(jnp.float32)

def rounded(values):
    return lax.optimization_barrier(values.astype(jnp.bfloat16)).astype(jnp.float32)

def window_scores(query_win, keys_win, table, onehot, shift_mask):
    raw = jnp.einsum('nabhid,nabhjd->nabhij', as_float(query_win), as_float(keys_win)) * HD ** (-0.5)
    bias = jnp.einsum('rh,ijr->hij', table, onehot, precision=lax.Precision.HIGHEST)
    return raw + bias[None, None, None] + shift_mask[None, :, :, None]

def attend_forward(query, keys, values, table, onehot, shift_mask, head_count):
    query_win = to_windows(query, head_count)
    keys_win = to_windows(keys, head_count)
    values_win = to_windows(values, head_count)
    scores = window_scores(query_win, keys_win, table, onehot, shift_mask)
    row_top = lax.optimization_barrier(jnp.max(scores, -1, keepdims=True))
    log_total = row_top + jnp.log(lax.optimization_barrier(jnp.sum(jnp.exp(scores - row_top), -1, keepdims=True)))
    probs = rounded(jnp.exp(scores - log_total))
    context = jnp.einsum('nabhij,nabhjd->nabhid', probs, as_float(values_win))
    return (from_windows(context).astype(jnp.bfloat16), log_total)

def attend_backward(query, keys, values, log_total, d_context, table, onehot, shift_mask, head_count):
    query_win = to_windows(query, head_count)
    keys_win = to_windows(keys, head_count)
    values_win = to_windows(values, head_count)
    scores = window_scores(query_win, keys_win, table, onehot, shift_mask)
    probs = jnp.exp(scores - log_total)
    d_win = as_float(to_windows(d_context, head_count))
    d_probs = jnp.einsum('nabhid,nabhjd->nabhij', d_win, as_float(values_win))
    d_values = jnp.einsum('nabhij,nabhid->nabhjd', rounded(probs), d_win)
    row_dot = lax.optimization_barrier(jnp.sum(probs * d_probs, -1, keepdims=True))
    d_scores = probs * (d_probs - row_dot)
    d_table = jnp.einsum('hij,ijr->rh', lax.optimization_barrier(jnp.sum(d_scores, (0, 1, 2))), onehot, precision=lax.Precision.HIGHEST)
    d_scores_low = rounded(d_scores)
    score_scale = HD ** (-0.5)
    d_query = jnp.einsum('nabhij,nabhjd->nabhid', d_scores_low, as_float(keys_win)) * score_scale
    d_keys = jnp.einsum('nabhij,nabhid->nabhjd', d_scores_low, as_float(query_win)) * score_scale
    return (from_windows(d_query), from_windows(d_keys), from_windows(d_values), d_table)

def layer_norm(rows, gain, shift):
    row_mean = lax.optimization_barrier(jnp.mean(rows, -1, keepdims=True))
    row_var = lax.optimization_barrier(jnp.mean(rows * rows, -1, keepdims=True)) - row_mean * row_mean
    inv_std = lax.rsqrt(row_var + eps_norm)
    normed = (rows - row_mean) * inv_std
    return (normed, inv_std, normed * gain + shift)

def norm_back(d_out, normed, inv_std, gain):
    d_normed = d_out * gain
    return inv_std * (d_normed - lax.optimization_barrier(jnp.mean(d_normed, -1, keepdims=True)) - normed * lax.optimization_barrier(jnp.mean(d_normed * normed, -1, keepdims=True)))

def gelu_parts(pre_act):
    cdf_part = 0.5 * (1.0 + jax.scipy.special.erf(pre_act * inv_root_two))
    return (pre_act * cdf_part, cdf_part + pre_act * jnp.exp(-0.5 * pre_act * pre_act) * inv_root_two_pi)

def matmul(left, right):
    return jnp.dot(left, right, preferred_element_type=jnp.float32)

def block_pass(x_rows, cot_rows, live_rows, params, onehot, shift_mask):
    ln1_gain, ln1_bias, qkv_weight, qv_bias, rel_table, proj_weight, proj_bias, ln2_gain, ln2_bias, fc1_weight, fc1_bias, fc2_weight, fc2_bias = params
    resid = x_rows.astype(jnp.float32)
    normed_one, scale_one, pre_one = layer_norm(resid, ln1_gain.astype(jnp.float32), ln1_bias.astype(jnp.float32))
    hidden_one = pre_one.astype(jnp.bfloat16)
    qkv_flat = qkv_weight.reshape(C, 3 * C)
    mixed = matmul(hidden_one, qkv_flat).reshape(-1, 3, C)
    bias_pair = qv_bias.astype(jnp.float32)
    query = (mixed[:, 0] + bias_pair[0]).astype(jnp.bfloat16)
    keys = mixed[:, 1].astype(jnp.bfloat16)
    values = (mixed[:, 2] + bias_pair[1]).astype(jnp.bfloat16)
    table = rel_table.astype(jnp.float32)
    context, log_total = attend_forward(query, keys, values, table, onehot, shift_mask, H)
    resid_one = resid + matmul(context, proj_weight) + proj_bias.astype(jnp.float32)
    normed_two, scale_two, pre_two = layer_norm(resid_one, ln2_gain.astype(jnp.float32), ln2_bias.astype(jnp.float32))
    hidden_two = pre_two.astype(jnp.bfloat16)
    pre_act = matmul(hidden_two, fc1_weight) + fc1_bias.astype(jnp.float32)
    act_full, slope = gelu_parts(pre_act)
    act_low = act_full.astype(jnp.bfloat16)
    output_rows = (resid_one + matmul(act_low, fc2_weight) + fc2_bias.astype(jnp.float32)).astype(jnp.bfloat16)
    grad_out = jnp.where(live_rows[:, None], cot_rows, jnp.zeros_like(cot_rows))
    grad_float = grad_out.astype(jnp.float32)
    d_fc2_bias = lax.optimization_barrier(jnp.sum(grad_float, 0))
    d_fc2_weight = matmul(act_low.T, grad_out)
    d_pre = matmul(grad_out, fc2_weight.T) * slope
    d_fc1_bias = lax.optimization_barrier(jnp.sum(d_pre, 0))
    d_pre_low = d_pre.astype(jnp.bfloat16)
    d_fc1_weight = matmul(hidden_two.T, d_pre_low)
    d_hidden_two = matmul(d_pre_low, fc1_weight.T)
    d_ln2_gain = lax.optimization_barrier(jnp.sum(d_hidden_two * normed_two, 0))
    d_ln2_bias = lax.optimization_barrier(jnp.sum(d_hidden_two, 0))
    d_resid_one = grad_float + norm_back(d_hidden_two, normed_two, scale_two, ln2_gain.astype(jnp.float32))
    d_proj_bias = lax.optimization_barrier(jnp.sum(d_resid_one, 0))
    d_resid_low = d_resid_one.astype(jnp.bfloat16)
    d_proj_weight = matmul(context.T, d_resid_low)
    d_context = matmul(d_resid_low, proj_weight.T).astype(jnp.bfloat16)
    d_query, d_keys, d_values, d_table = attend_backward(query, keys, values, log_total, d_context, table, onehot, shift_mask, H)
    d_qv_bias = jnp.stack([lax.optimization_barrier(jnp.sum(d_query, 0)), lax.optimization_barrier(jnp.sum(d_values, 0))])
    d_mixed = jnp.stack([d_query, d_keys, d_values], 1).astype(jnp.bfloat16).reshape(-1, 3 * C)
    d_qkv_weight = matmul(hidden_one.T, d_mixed).reshape(C, 3, C)
    d_hidden_one = matmul(d_mixed, qkv_flat.T)
    d_ln1_gain = lax.optimization_barrier(jnp.sum(d_hidden_one * normed_one, 0))
    d_ln1_bias = lax.optimization_barrier(jnp.sum(d_hidden_one, 0))
    d_rows = (d_resid_one + norm_back(d_hidden_one, normed_one, scale_one, ln1_gain.astype(jnp.float32))).astype(jnp.bfloat16)
    grads = (d_ln1_gain, d_ln1_bias, d_qkv_weight, d_qv_bias, d_table, d_proj_weight, d_proj_bias, d_ln2_gain, d_ln2_bias, d_fc1_weight, d_fc1_bias, d_fc2_weight, d_fc2_bias)
    return (output_rows, d_rows, grads)

def add_pair(left, right):
    return left + right

def reference(block_input, cotangent, live_images, ln1_gain, ln1_bias, qkv_weight, qv_bias, rel_table, proj_weight, proj_bias, ln2_gain, ln2_bias, fc1_weight, fc1_bias, fc2_weight, fc2_bias):
    onehot, shift_mask = window_tables()
    params = (ln1_gain, ln1_bias, qkv_weight, qv_bias, rel_table, proj_weight, proj_bias, ln2_gain, ln2_bias, fc1_weight, fc1_bias, fc2_weight, fc2_bias)
    block_tokens = IMG_DEV * GRID * GRID
    slot_index = (jnp.arange(block_tokens, dtype=jnp.int32) // (GRID * GRID)).astype(jnp.int32)
    x_blocks = block_input.reshape(N_GX, block_tokens, C)
    cot_blocks = cotangent.reshape(N_GX, block_tokens, C)

    def step_block(carry, inputs):
        x_rows, cot_rows, count = inputs
        live_rows = slot_index < count
        output_rows, d_rows, grads = block_pass(x_rows, cot_rows, live_rows, params, onehot, shift_mask)
        return (jax.tree.map(add_pair, carry, grads), (output_rows, d_rows))
    zeros = tuple((jnp.zeros(param.shape, jnp.float32) for param in params))
    totals, (outputs, d_inputs) = lax.scan(step_block, zeros, (x_blocks, cot_blocks, live_images.astype(jnp.int32)))
    return (outputs.reshape(TOKENS, C), d_inputs.reshape(TOKENS, C), totals[0], totals[1], totals[2], totals[3], totals[4], totals[5], totals[6], totals[7], totals[8], totals[9], totals[10], totals[11], totals[12])
```

```python
import functools
import jax
import jax.numpy as jnp
from jax import lax
import numpy as np
from jax.experimental import pallas as pl
from jax.experimental.pallas import tpu as pltpu
from jax.sharding import PartitionSpec as P

HD = 32
GRID = 14
WIN = 7
SHIFT = 3
RELS = 169


eps_norm = 1e-05
mask_value = -100.0
inv_root_two = 0.7071067811865476
inv_root_two_pi = 0.3989422804014327


def matmul(left, right):
    return jnp.dot(left, right, preferred_element_type=jnp.float32)


def matmul_tn(left, right):
    return lax.dot_general(
        left, right, (((0,), (0,)), ((), ())), preferred_element_type=jnp.float32
    )


def matmul_nt(left, right):
    return lax.dot_general(
        left, right, (((1,), (1,)), ((), ())), preferred_element_type=jnp.float32
    )


SLOT = 64
PACK = 8
WIN_COUNT = (GRID // WIN) ** 2
IMAGE = GRID * GRID
ALIGN = 16
STEP = IMAGE // ALIGN * ALIGN
SPAN = STEP + ALIGN
far_below = -1e30


def static_tables(image_count):
    rows = np.arange(WIN_COUNT * SLOT)
    win, place = rows // SLOT, rows % SLOT
    row = (win // (GRID // WIN) * WIN + place // WIN + SHIFT) % GRID
    col = (win % (GRID // WIN) * WIN + place % WIN + SHIFT) % GRID
    token = np.where(place < WIN * WIN, row * GRID + col, -1)
    offset = np.arange(image_count) * (IMAGE - STEP)
    column = np.where(token[None] >= 0, token[None] + offset[:, None], -1)
    places = np.arange(SLOT)
    live = places < WIN * WIN
    pr, pc = places // WIN, places % WIN
    rel = (pr[None, :] - pr[:, None] + WIN - 1) * (2 * WIN - 1) + pc[None, :] - pc[:, None] + WIN - 1
    rel = np.where(live[:, None] & live[None, :], rel, -1)
    cells = np.arange(GRID)
    region = np.where(cells < GRID - WIN, 0, np.where(cells < GRID - SHIFT, 1, 2))
    shifted_row = (win // (GRID // WIN) * WIN + np.minimum(place // WIN, WIN - 1)).reshape(WIN_COUNT, SLOT)
    shifted_col = (win % (GRID // WIN) * WIN + place % WIN).reshape(WIN_COUNT, SLOT)
    ids = region[shifted_row] * 3 + region[shifted_col]
    mask = np.where(ids[:, :, None] == ids[:, None, :], 0.0, mask_value)
    mask = np.where(live[None, None, :] & live[None, :, None], mask, 0.0)
    mask = np.where(live[None, :, None], mask, far_below)
    return column.astype(np.int32), rel.astype(np.int32), mask.astype(np.float32)


def attention_tables(rel_table, image_count):
    column, rel, mask = static_tables(image_count)
    spots = np.arange(SPAN, dtype=np.int32)
    perm = jnp.asarray((column[:, :, None] == spots).astype(np.float32)).astype(jnp.bfloat16)
    perm_t = jnp.asarray((column[:, None, :] == spots[:, None]).astype(np.float32)).astype(jnp.bfloat16)
    heads = rel_table.shape[0]
    onehot = (jnp.arange(RELS, dtype=jnp.int32)[:, None] == jnp.asarray(rel.reshape(1, -1))).astype(
        jnp.bfloat16
    )
    bias = lax.dot_general(
        rel_table, onehot, (((1,), (0,)), ((), ())), preferred_element_type=jnp.float32
    )
    bias = bias.reshape(heads // PACK, PACK, SLOT, SLOT).transpose(0, 2, 1, 3)
    bias = bias[None] + jnp.asarray(mask)[:, None, :, None, :]
    bias = bias.reshape(WIN_COUNT, heads // PACK, SLOT, PACK * SLOT)
    owner = np.arange(PACK * SLOT)[:, None] // SLOT == np.arange(PACK * HD)[None, :] // HD
    owner = jnp.asarray(owner.astype(np.float32)).astype(jnp.bfloat16)
    return perm, perm_t, bias, owner, onehot


def spread(rows, owner):
    return jnp.concatenate([rows] * PACK, axis=0) * owner


def gather_heads(full):
    lanes = lax.broadcasted_iota(jnp.int32, (SLOT, PACK * HD), 1) // HD
    total = full[:SLOT]
    for h in range(1, PACK):
        total = jnp.where(lanes == h, full[h * SLOT : (h + 1) * SLOT], total)
    return total


def forward_kernel(qkv_ref, perm_ref, perm_t_ref, bias_ref, owner_ref, context_ref, windows_ref, probs_ref, ctx_ref):
    image = pl.program_id(0)
    width = context_ref.shape[1]
    groups = width // (PACK * HD)
    start = pl.multiple_of(image * STEP, ALIGN)
    windows_ref[0] = matmul(perm_ref[0], qkv_ref[pl.ds(start, SPAN), :]).astype(jnp.bfloat16)
    for w in range(WIN_COUNT):
        rows = slice(w * SLOT, (w + 1) * SLOT)
        for g in range(groups):
            low = g * PACK * HD
            query = windows_ref[0, rows, low : low + PACK * HD]
            keys = windows_ref[0, rows, width + low : width + low + PACK * HD]
            values = windows_ref[0, rows, 2 * width + low : 2 * width + low + PACK * HD]
            scores = matmul_nt(keys, spread(query, owner_ref[...])) * HD ** (-0.5) + bias_ref[w, g]
            raised = jnp.exp(scores - jnp.max(scores, 0, keepdims=True))
            probs = raised * (1.0 / jnp.sum(raised, 0, keepdims=True))
            probs_ref[0, w * groups + g] = probs
            full = matmul_tn(probs.astype(jnp.bfloat16), values)
            ctx_ref[rows, low : low + PACK * HD] = gather_heads(full).astype(jnp.bfloat16)

    @pl.when(image == 0)
    def _():
        context_ref[...] = jnp.zeros_like(context_ref)

    context_ref[pl.ds(start, SPAN), :] += matmul(perm_t_ref[0], ctx_ref[...]).astype(jnp.bfloat16)


def backward_kernel(
    d_context_ref, windows_ref, probs_ref, perm_ref, perm_t_ref, owner_ref,
    d_mixed_ref, d_bias_ref, d_qv_ref, d_ctx_ref, d_win_ref,
):
    image = pl.program_id(0)
    width = d_context_ref.shape[1]
    groups = width // (PACK * HD)
    start = pl.multiple_of(image * STEP, ALIGN)

    @pl.when(image == 0)
    def _():
        d_mixed_ref[...] = jnp.zeros_like(d_mixed_ref)
        d_bias_ref[...] = jnp.zeros_like(d_bias_ref)
        d_qv_ref[...] = jnp.zeros_like(d_qv_ref)

    d_ctx_ref[...] = matmul(perm_ref[0], d_context_ref[pl.ds(start, SPAN), :]).astype(jnp.bfloat16)
    for g in range(groups):
        low = g * PACK * HD
        cols = slice(low, low + PACK * HD)
        d_bias = jnp.zeros((SLOT, PACK * SLOT), jnp.float32)
        d_query_sum = jnp.zeros((1, PACK * HD), jnp.float32)
        d_value_sum = jnp.zeros((1, PACK * HD), jnp.float32)
        for w in range(WIN_COUNT):
            rows = slice(w * SLOT, (w + 1) * SLOT)
            query = windows_ref[0, rows, low : low + PACK * HD]
            keys = windows_ref[0, rows, width + low : width + low + PACK * HD]
            values = windows_ref[0, rows, 2 * width + low : 2 * width + low + PACK * HD]
            probs = probs_ref[0, w * groups + g]
            d_wide = spread(d_ctx_ref[rows, cols], owner_ref[...])
            d_probs = matmul_nt(values, d_wide)
            d_values = matmul(probs.astype(jnp.bfloat16), d_wide)
            d_scores = probs * (d_probs - jnp.sum(probs * d_probs, 0, keepdims=True))
            d_bias = d_bias + d_scores
            d_low = d_scores.astype(jnp.bfloat16)
            d_keys = matmul(d_low, spread(query, owner_ref[...])) * HD ** (-0.5)
            d_query = gather_heads(matmul_tn(d_low, keys)) * HD ** (-0.5)
            d_win_ref[rows, low : low + PACK * HD] = d_query.astype(jnp.bfloat16)
            d_win_ref[rows, width + low : width + low + PACK * HD] = d_keys.astype(jnp.bfloat16)
            d_win_ref[rows, 2 * width + low : 2 * width + low + PACK * HD] = d_values.astype(jnp.bfloat16)
            d_query_sum = d_query_sum + jnp.sum(d_query, 0, keepdims=True)
            d_value_sum = d_value_sum + jnp.sum(d_values, 0, keepdims=True)
        d_bias_ref[g] += d_bias
        d_qv_ref[0:1, cols] += d_query_sum
        d_qv_ref[1:2, cols] += d_value_sum
    d_mixed_ref[pl.ds(start, SPAN), :] += matmul(perm_t_ref[0], d_win_ref[...]).astype(jnp.bfloat16)


def whole(shape):
    return pl.BlockSpec(shape, lambda n: (0,) * len(shape))


def per_image(shape):
    return pl.BlockSpec((1,) + shape, lambda n: (n,) + (0,) * len(shape))


def attend_forward(qkv, tables):
    perm, perm_t, bias, owner, _ = tables
    tok, wide = qkv.shape
    width = wide // 3
    count, spots = perm.shape[:2]
    tiles = WIN_COUNT * width // (PACK * HD)
    return pl.pallas_call(
        forward_kernel,
        grid=(count,),
        in_specs=[whole(qkv.shape), per_image((spots, SPAN)), per_image((SPAN, spots)), whole(bias.shape), whole(owner.shape)],
        out_specs=[whole((tok, width)), per_image((spots, wide)), per_image((tiles, SLOT, PACK * SLOT))],
        out_shape=[
            jax.ShapeDtypeStruct((tok, width), jnp.bfloat16),
            jax.ShapeDtypeStruct((count, spots, wide), jnp.bfloat16),
            jax.ShapeDtypeStruct((count, tiles, SLOT, PACK * SLOT), jnp.float32),
        ],
        scratch_shapes=[pltpu.VMEM((spots, width), jnp.bfloat16)],
        cost_estimate=pl.CostEstimate(flops=6_000_000_000, bytes_accessed=24_000_000, transcendentals=tok * width * 2),
        name="attend_forward",
    )(qkv, perm, perm_t, bias, owner)


def attend_backward(d_context, windows, probs, tables):
    perm, perm_t, _, owner, onehot = tables
    tok, width = d_context.shape
    count, spots, wide = windows.shape
    groups = width // (PACK * HD)
    tiles = probs.shape[1]
    d_mixed, d_bias, d_qv = pl.pallas_call(
        backward_kernel,
        grid=(count,),
        in_specs=[
            whole(d_context.shape), per_image((spots, wide)), per_image((tiles, SLOT, PACK * SLOT)),
            per_image((spots, SPAN)), per_image((SPAN, spots)), whole(owner.shape),
        ],
        out_specs=[whole((tok, wide)), whole((groups, SLOT, PACK * SLOT)), whole((2, width))],
        out_shape=[
            jax.ShapeDtypeStruct((tok, wide), jnp.bfloat16),
            jax.ShapeDtypeStruct((groups, SLOT, PACK * SLOT), jnp.float32),
            jax.ShapeDtypeStruct((2, width), jnp.float32),
        ],
        scratch_shapes=[pltpu.VMEM((spots, width), jnp.bfloat16), pltpu.VMEM((spots, wide), jnp.bfloat16)],
        cost_estimate=pl.CostEstimate(flops=9_000_000_000, bytes_accessed=32_000_000, transcendentals=0),
        name="attend_backward",
    )(d_context, windows, probs, perm, perm_t, owner)
    d_bias = d_bias.reshape(groups, SLOT, PACK, SLOT).transpose(0, 2, 1, 3).reshape(groups * PACK, SLOT * SLOT)
    d_table = lax.dot_general(
        onehot.astype(jnp.float32), d_bias, (((1,), (1,)), ((), ())), precision=lax.Precision.HIGHEST
    )
    return d_mixed, d_qv, d_table


def gelu_parts(pre_act):
    cdf_part = 0.5 * (1.0 + jax.scipy.special.erf(pre_act * inv_root_two))
    return (
        pre_act * cdf_part,
        cdf_part + pre_act * jnp.exp(-0.5 * pre_act * pre_act) * inv_root_two_pi,
    )


def layer_norm(rows, gain, shift):
    row_mean = jnp.mean(rows, -1, keepdims=True)
    row_var = jnp.mean(rows * rows, -1, keepdims=True) - row_mean * row_mean
    inv_std = lax.rsqrt(row_var + eps_norm)
    normed = (rows - row_mean) * inv_std
    return (normed, inv_std, normed * gain + shift)


def norm_back(d_out, normed, inv_std, gain):
    d_normed = d_out * gain
    return inv_std * (
        d_normed
        - jnp.mean(d_normed, -1, keepdims=True)
        - normed * jnp.mean(d_normed * normed, -1, keepdims=True)
    )


ROW_PAD = 16


def bit_of(index, bit):
    return (index // (1 << bit)) % 2


def bits_of(size):
    return size.bit_length() - 1


def greet(gx_size, gy_size):
    mine, row = lax.axis_index("gx"), lax.axis_index("gy")
    barrier = pltpu.get_barrier_semaphore()
    for name, index, size in (("gx", mine, gx_size), ("gy", row, gy_size)):
        for bit in range(bits_of(size)):
            there = index + (1 << bit) * (1 - 2 * bit_of(index, bit))
            pl.semaphore_signal(barrier, inc=1, device_id={name: there}, device_id_type=pl.DeviceIdType.MESH)
    pl.semaphore_wait(barrier, bits_of(gx_size) + bits_of(gy_size))


class Sender:
    def __init__(self, send, recv):
        self.send, self.recv, self.used = send, recv, 0

    def start(self, src, dst, name, there):
        copy = pltpu.make_async_remote_copy(
            src_ref=src,
            dst_ref=dst,
            send_sem=self.send.at[self.used],
            recv_sem=self.recv.at[self.used],
            device_id={name: there},
            device_id_type=pl.DeviceIdType.MESH,
        )
        self.used += 1
        copy.start()
        return copy


def split_steps(index, size):
    top = bits_of(size) - 1
    core = index % 2
    high, low = bit_of(index, top), bit_of(index, top - 1)
    big, small = 1 << top, 1 << (top - 1)
    first_step = (1 - core) * big * (1 - 2 * high) + core * small * (1 - 2 * low)
    second_step = (1 - core) * small * (1 - 2 * low) + core * big * (1 - 2 * high)
    return core, high, low, first_step, second_step


def gather_column(sender, local, slots, sizes, sem):
    gy_size = sizes[1]
    row = lax.axis_index("gy")
    own = [pltpu.make_async_copy(ref, slot.at[row], sem.at[n]) for n, (ref, slot) in enumerate(zip(local, slots))]
    for copy in own:
        copy.start()
    held = [row]
    for bit in range(bits_of(gy_size))[::-1]:
        step = (1 << bit) * (1 - 2 * bit_of(row, bit))
        copies = [
            sender.start(local[n] if place == 0 else slot.at[at], slot.at[at], "gy", row + step)
            for place, at in enumerate(held)
            for n, slot in enumerate(slots)
        ]
        yield
        for copy in copies:
            copy.wait()
        held = held + [at + step for at in held]
    for copy in own:
        copy.wait()


def join_rows(slots, full, groups):
    mine = lax.axis_index("gx")
    gy_size, rows, wide = slots.shape
    width = wide // groups
    at = pl.multiple_of(mine * rows, rows)
    for i in range(gy_size):
        for k in range(groups):
            low = (k * gy_size + i) * width
            full[pl.ds(at, rows), low : low + width] = slots[i, :, k * width : (k + 1) * width]


def gather_plane(sender, fulls, sizes):
    gx_size = sizes[0]
    mine = lax.axis_index("gx")
    core, _, _, first_step, second_step = split_steps(mine, gx_size)
    steps = [first_step, second_step]
    for bit in range(1, bits_of(gx_size) - 2)[::-1]:
        steps.append((1 << bit) * (1 - 2 * bit_of(mine, bit)))
    over = 1 - 2 * core

    def push(at, there):
        out = []
        for full in fulls:
            rows = full.shape[0] // gx_size
            view = full.at[pl.ds(pl.multiple_of(at * rows, rows), rows), :]
            out.append(sender.start(view, view, "gx", there))
        return out

    held = [mine]
    shared = []
    fresh = [mine]
    for step in steps:
        copies = [copy for at in held for copy in push(at, mine + step)]
        shared += [copy for at in fresh for copy in push(at, mine + over)]
        yield
        for copy in copies:
            copy.wait()
        fresh = [at + step for at in held]
        held = held + fresh
    shared += [copy for at in fresh for copy in push(at, mine + over)]
    yield
    for copy in shared:
        copy.wait()


def run_all(*streams):
    for stream in streams:
        for _ in stream:
            pass


def advance(stream, count=1):
    for _ in range(count):
        next(stream, None)


def gather_kernel(sizes, qkv_ref, proj_ref, small_ref, fc1_ref, fc2_ref, qkv_full, proj_full, fc1_full, fc2_full, small_all,
                  qkv_slots, proj_slots, fc1_slots, fc2_slots, send, recv, own_sem):
    gx_size, gy_size = sizes
    greet(gx_size, gy_size)
    sender = Sender(send, recv)

    def early():
        yield from gather_column(sender, [qkv_ref, proj_ref, small_ref], [qkv_slots, proj_slots, small_all], sizes, own_sem.at[0])
        join_rows(qkv_slots, qkv_full, 3)
        join_rows(proj_slots, proj_full, 1)
        yield from gather_plane(sender, [qkv_full, proj_full], sizes)

    def later():
        yield from gather_column(sender, [fc1_ref, fc2_ref], [fc1_slots, fc2_slots], sizes, own_sem.at[1])
        join_rows(fc1_slots, fc1_full, 1)
        join_rows(fc2_slots, fc2_full, 1)
        yield from gather_plane(sender, [fc1_full, fc2_full], sizes)

    first, second = early(), later()
    advance(first, 2)
    advance(second)
    while True:
        done = next(first, "done")
        advance(second)
        if done == "done":
            break
    run_all(second)


def vmem_spec():
    return pl.BlockSpec(memory_space=pltpu.VMEM)


def gather_weights(qkv, proj_t, small, fc1, fc2_t):
    sizes = (lax.axis_size("gx"), lax.axis_size("gy"))
    gx_size, gy_size = sizes
    rows = qkv.shape[0]
    full = [jax.ShapeDtypeStruct((rows * gx_size, v.shape[1] * gy_size), v.dtype) for v in (qkv, proj_t, fc1, fc2_t)]
    slots = [pltpu.VMEM((gy_size,) + v.shape, v.dtype) for v in (qkv, proj_t, fc1, fc2_t)]
    count = 5 * (gy_size - 1) + 4 * (gx_size - 1)
    return pl.pallas_call(
        functools.partial(gather_kernel, sizes),
        in_specs=[vmem_spec()] * 5,
        out_specs=[vmem_spec()] * 5,
        out_shape=full + [jax.ShapeDtypeStruct((gy_size,) + small.shape, small.dtype)],
        scratch_shapes=slots + [
            pltpu.SemaphoreType.DMA((count,)), pltpu.SemaphoreType.DMA((count,)), pltpu.SemaphoreType.DMA((2, 3)),
        ],
        compiler_params=pltpu.CompilerParams(collective_id=0, has_side_effects=True, vmem_limit_bytes=24 << 20),
        name="gather_weights",
    )(qkv, proj_t, small, fc1, fc2_t)


def add_into(target, left, right):
    target[...] = (left[...].astype(jnp.float32) + right[...].astype(jnp.float32)).astype(target.dtype)


def share_plane(sender, full, halves, sizes):
    gx_size = sizes[0]
    mine = lax.axis_index("gx")
    rows = full.shape[0] // gx_size
    core, high, low, first_step, second_step = split_steps(mine, gx_size)

    def block(at):
        return full.at[pl.ds(pl.multiple_of(at * rows, rows), rows), :]

    held = block
    count = gx_size
    for bit in range(bits_of(gx_size)):
        came = halves[bit]
        count //= 2
        own = bit_of(mine, bit)
        if count >= 4:
            step = (1 << bit) * (1 - 2 * own)
            away = [2 * k + 1 - own for k in range(count)]
            kept = [2 * k + own for k in range(count)]
        elif count == 2:
            step = second_step
            away = [(1 - core) * (2 * k + 1 - low) + core * (2 * (1 - high) + k) for k in range(count)]
            kept = [(1 - core) * (2 * k + low) + core * (2 * high + k) for k in range(count)]
        else:
            step = first_step
            last = (1 - core) * high + core * low
            away, kept = [1 - last], [last]
        copies = [sender.start(held(at), came.at[k], "gx", mine + step) for k, at in enumerate(away)]
        yield
        for k, at in enumerate(kept):
            copies[k].wait()
            add_into(came.at[k], came.at[k], held(at))
        held = (lambda ref: lambda at: ref.at[at])(came)


def share_column(sender, total, slots, halves, out, groups, sizes):
    gy_size = sizes[1]
    row = lax.axis_index("gy")
    width = slots.shape[2] // groups
    for i in range(gy_size):
        for k in range(groups):
            low = (k * gy_size + i) * width
            slots[i, :, k * width : (k + 1) * width] = total[0, :, low : low + width]
    held = slots
    count = gy_size
    for bit in range(bits_of(gy_size)):
        came = halves[bit]
        count //= 2
        own = bit_of(row, bit)
        step = (1 << bit) * (1 - 2 * own)
        copies = [sender.start(held.at[2 * k + 1 - own], came.at[k], "gy", row + step) for k in range(count)]
        yield
        for k in range(count):
            copies[k].wait()
            if count == 1:
                add_into(out, came.at[0], held.at[own])
            else:
                add_into(came.at[k], came.at[k], held.at[2 * k + own])
        held = came


def sum_small(sender, value, came, totals, out, sizes):
    held = value
    stage = 0
    stages = bits_of(sizes[0]) + bits_of(sizes[1])
    for name, size in (("gx", sizes[0]), ("gy", sizes[1])):
        index = lax.axis_index(name)
        for bit in range(bits_of(size)):
            there = index + (1 << bit) * (1 - 2 * bit_of(index, bit))
            copy = sender.start(held, came.at[stage], name, there)
            yield
            copy.wait()
            target = out if stage == stages - 1 else totals.at[stage]
            target[...] = held[...] + came[stage]
            held = target
            stage += 1


def share_kernel(sizes, groups, *refs):
    gx_size, gy_size = sizes
    arrays = len(groups)
    gx_bits, gy_bits = bits_of(gx_size), bits_of(gy_size)
    refs = list(refs)

    def take(count):
        out = refs[:count]
        del refs[:count]
        return out

    fulls, (small,) = take(arrays), take(1)
    outs, (small_out,) = take(arrays), take(1)
    planes = [take(gx_bits) for _ in range(arrays)]
    slots = take(arrays)
    columns = [take(gy_bits) for _ in range(arrays)]
    small_came, small_totals, send, recv = take(4)
    greet(gx_size, gy_size)
    sender = Sender(send, recv)

    def one(n):
        yield from share_plane(sender, fulls[n], planes[n], sizes)
        yield from share_column(sender, planes[n][-1], slots[n], columns[n], outs[n], groups[n], sizes)

    streams = [one(n) for n in range(arrays)] + [sum_small(sender, small, small_came, small_totals, small_out, sizes)]
    for _ in range(gx_bits + gy_bits + 1):
        for stream in streams:
            next(stream, None)


def share_sums(fulls, groups, small):
    sizes = (lax.axis_size("gx"), lax.axis_size("gy"))
    gx_size, gy_size = sizes
    gx_bits, gy_bits = bits_of(gx_size), bits_of(gy_size)
    rows = fulls[0].shape[0] // gx_size
    planes, slots, columns = [], [], []
    for full in fulls:
        wide = full.shape[1]
        planes += [pltpu.VMEM((gx_size >> (bit + 1), rows, wide), full.dtype) for bit in range(gx_bits)]
        slots.append(pltpu.VMEM((gy_size, rows, wide // gy_size), full.dtype))
        columns += [pltpu.VMEM((gy_size >> (bit + 1), rows, wide // gy_size), full.dtype) for bit in range(gy_bits)]
    stages = gx_bits + gy_bits
    count = len(fulls) * (gx_size - 1 + gy_size - 1) + stages
    return pl.pallas_call(
        functools.partial(share_kernel, sizes, groups),
        in_specs=[vmem_spec()] * (len(fulls) + 1),
        out_specs=[vmem_spec()] * (len(fulls) + 1),
        out_shape=[jax.ShapeDtypeStruct((rows, full.shape[1] // gy_size), jnp.float32) for full in fulls]
        + [jax.ShapeDtypeStruct(small.shape, small.dtype)],
        scratch_shapes=planes + slots + columns + [
            pltpu.VMEM((stages,) + small.shape, small.dtype),
            pltpu.VMEM((stages,) + small.shape, small.dtype),
            pltpu.SemaphoreType.DMA((count,)),
            pltpu.SemaphoreType.DMA((count,)),
        ],
        compiler_params=pltpu.CompilerParams(collective_id=1, has_side_effects=True, vmem_limit_bytes=40 << 20),
        name="share_sums",
    )(*fulls, small)


def pack_rows(values):
    rows = []
    for value in values:
        flat = value.reshape(-1)
        rows.append(jnp.pad(flat, (0, -flat.shape[0] % 1024)).reshape(-1, 128))
    return jnp.concatenate(rows, 0)


def unpack_rows(packed, shapes):
    at, out = 0, []
    for shape in shapes:
        size = int(np.prod(shape))
        count = (size + 1023) // 1024 * 8
        out.append(packed[at : at + count].reshape(-1)[:size].reshape(shape))
        at += count
    return out


def own_columns(summed, axis):
    size = summed.shape[axis] // lax.axis_size("gy")
    return lax.dynamic_slice_in_dim(summed, lax.axis_index("gy") * size, size, axis)


def local_live(tok_local, live_images):
    position = lax.axis_index("gy")
    per_device = tok_local // (GRID * GRID)
    slot_index = position * per_device + jnp.arange(tok_local, dtype=jnp.int32) // (GRID * GRID)
    return slot_index < live_images[0]


def blocked_layer(block_input, cotangent, live_images, params):
    (
        ln1_gain,
        ln1_bias,
        qkv_weight,
        qv_bias,
        rel_table,
        proj_weight,
        proj_bias,
        ln2_gain,
        ln2_bias,
        fc1_weight,
        fc1_bias,
        fc2_weight,
        fc2_bias,
    ) = params
    tok_local, width = block_input.shape
    block_rows = qkv_weight.shape[0]
    part, hidden_local = qkv_weight.shape[2], fc1_weight.shape[1]
    heads_local = rel_table.shape[1]

    def lane_row(value):
        value = value.reshape(value.shape[0], -1)
        return jnp.pad(value, ((0, 0), (0, hidden_local - value.shape[1])))

    small = jnp.concatenate([fc1_bias[None], lane_row(qv_bias.reshape(1, -1)), lane_row(rel_table.T)], 0)
    small = jnp.pad(small, ((0, ROW_PAD - small.shape[0]), (0, 0)))
    qkv_flat, proj_cols, fc1_rows, fc2_cols, small = gather_weights(
        qkv_weight.reshape(block_rows, -1), proj_weight.T, small, fc1_weight, fc2_weight.T
    )
    fc1_bias = small[:, 0].reshape(-1)
    qv_bias = small[:, 1, : 2 * part].reshape(-1, 2, part).transpose(1, 0, 2).reshape(2, -1)
    rel_table = small[:, 2 : 2 + heads_local, :RELS].reshape(-1, RELS)
    gain_one = ln1_gain.astype(jnp.float32)
    gain_two = ln2_gain.astype(jnp.float32)
    resid = block_input.astype(jnp.float32)
    normed_one, scale_one, pre_one = layer_norm(resid, gain_one, ln1_bias.astype(jnp.float32))
    hidden_one = (pre_one.astype(jnp.bfloat16))
    bias_row = jnp.stack([qv_bias[0], jnp.zeros_like(qv_bias[0]), qv_bias[1]]).reshape(1, 3 * width)
    mixed = (matmul(hidden_one, qkv_flat) + bias_row.astype(jnp.float32)).astype(jnp.bfloat16)
    tables = attention_tables(rel_table, tok_local // IMAGE)
    context, windows, probs = attend_forward(mixed, tables)
    resid_one = resid + (matmul_nt(context, proj_cols)) + proj_bias.astype(jnp.float32)
    normed_two, scale_two, pre_two = layer_norm(resid_one, gain_two, ln2_bias.astype(jnp.float32))
    hidden_two = (pre_two.astype(jnp.bfloat16))
    pre_act = matmul(hidden_two, fc1_rows) + fc1_bias.astype(jnp.float32)
    act_full, slope = gelu_parts(pre_act)
    act_low = act_full.astype(jnp.bfloat16)
    output = (
        resid_one + (matmul_nt(act_low, fc2_cols)) + fc2_bias.astype(jnp.float32)
    ).astype(jnp.bfloat16)
    live_rows = local_live(tok_local, live_images)
    grad_out = jnp.where(live_rows[:, None], cotangent, jnp.zeros_like(cotangent))
    grad_float = grad_out.astype(jnp.float32)
    grad_full = (grad_out)
    d_fc2_bias = jnp.sum(grad_float, 0)
    d_fc2_weight = matmul_tn(grad_full, act_low).astype(jnp.bfloat16)
    d_pre = matmul(grad_full, fc2_cols) * slope
    d_fc1_bias = jnp.sum(d_pre, 0)
    d_pre_low = d_pre.astype(jnp.bfloat16)
    d_fc1_weight = matmul_tn(hidden_two, d_pre_low).astype(jnp.bfloat16)
    d_hidden_two = (matmul_nt(d_pre_low, fc1_rows))
    d_ln2_gain = jnp.sum(d_hidden_two * normed_two, 0)
    d_ln2_bias = jnp.sum(d_hidden_two, 0)
    d_resid_one = grad_float + norm_back(d_hidden_two, normed_two, scale_two, gain_two)
    d_proj_bias = jnp.sum(d_resid_one, 0)
    d_resid_full = (d_resid_one.astype(jnp.bfloat16))
    d_proj_weight = matmul_tn(d_resid_full, context).astype(jnp.bfloat16)
    d_context = matmul(d_resid_full, proj_cols).astype(jnp.bfloat16)
    d_mixed, d_qv_bias, d_table = attend_backward(d_context, windows, probs, tables)
    d_qkv_weight = matmul_tn(hidden_one, d_mixed).astype(jnp.bfloat16)
    d_hidden_one = (matmul_nt(d_mixed, qkv_flat))
    d_ln1_gain = jnp.sum(d_hidden_one * normed_one, 0)
    d_ln1_bias = jnp.sum(d_hidden_one, 0)
    d_input = (d_resid_one + norm_back(d_hidden_one, normed_one, scale_one, gain_one)).astype(
        jnp.bfloat16
    )
    own = (d_ln1_gain, d_ln1_bias, d_proj_bias, d_ln2_gain, d_ln2_bias, d_fc2_bias, d_qv_bias, d_table, d_fc1_bias)
    d_fc1_weight, d_fc2_weight, d_qkv_weight, d_proj_weight, sums = share_sums(
        (d_fc1_weight, d_fc2_weight, d_qkv_weight, d_proj_weight), (1, 1, 3, 1), pack_rows(own)
    )
    d_fc2_weight = d_fc2_weight.T
    d_proj_weight = d_proj_weight.T
    d_qkv_weight = d_qkv_weight.reshape(block_rows, 3, part)
    sums = unpack_rows(sums, [value.shape for value in own])
    norm_sums = sums[:6]
    head_sums = (own_columns(sums[6], 1), own_columns(sums[7], 1), own_columns(sums[8], 0))
    return (
        output,
        d_input,
        norm_sums[0],
        norm_sums[1],
        d_qkv_weight,
        head_sums[0],
        head_sums[1],
        d_proj_weight,
        norm_sums[2],
        norm_sums[3],
        norm_sums[4],
        d_fc1_weight,
        head_sums[2],
        d_fc2_weight,
        norm_sums[5],
    )


def shards(
    block_input,
    cotangent,
    live_images,
    ln1_gain,
    ln1_bias,
    qkv_weight,
    qv_bias,
    rel_table,
    proj_weight,
    proj_bias,
    ln2_gain,
    ln2_bias,
    fc1_weight,
    fc1_bias,
    fc2_weight,
    fc2_bias,
):
    params = (
        ln1_gain,
        ln1_bias,
        qkv_weight,
        qv_bias,
        rel_table,
        proj_weight,
        proj_bias,
        ln2_gain,
        ln2_bias,
        fc1_weight,
        fc1_bias,
        fc2_weight,
        fc2_bias,
    )
    return blocked_layer(block_input, cotangent, live_images, params)


def solution(mesh):
    return jax.shard_map(
        shards,
        mesh=mesh,
        in_specs=(
            P(("gx", "gy"), None),
            P(("gx", "gy"), None),
            P("gx"),
            P(),
            P(),
            P("gx", None, "gy"),
            P(None, "gy"),
            P(None, "gy"),
            P("gy", "gx"),
            P(),
            P(),
            P(),
            P("gx", "gy"),
            P("gy"),
            P("gy", "gx"),
            P(),
        ),
        out_specs=(
            P(("gx", "gy"), None),
            P(("gx", "gy"), None),
            P(),
            P(),
            P("gx", None, "gy"),
            P(None, "gy"),
            P(None, "gy"),
            P("gy", "gx"),
            P(),
            P(),
            P(),
            P("gx", "gy"),
            P("gy"),
            P("gy", "gx"),
            P(),
        ),
        check_vma=False,
    )
```

```python
import functools
import jax
import jax.numpy as jnp
from jax import lax
import numpy as np
from jax.experimental import pallas as pl
from jax.experimental.pallas import tpu as pltpu
from jax.sharding import PartitionSpec as P

HD = 32
GRID = 14
WIN = 7
SHIFT = 3
RELS = 169


eps_norm = 1e-05
mask_value = -100.0
inv_root_two = 0.7071067811865476
inv_root_two_pi = 0.3989422804014327


def matmul(left, right):
    return jnp.dot(left, right, preferred_element_type=jnp.float32)


def matmul_tn(left, right):
    return lax.dot_general(
        left, right, (((0,), (0,)), ((), ())), preferred_element_type=jnp.float32
    )


def matmul_nt(left, right):
    return lax.dot_general(
        left, right, (((1,), (1,)), ((), ())), preferred_element_type=jnp.float32
    )


SLOT = 64
PACK = 8
WIN_COUNT = (GRID // WIN) ** 2
IMAGE = GRID * GRID
ALIGN = 16
STEP = IMAGE // ALIGN * ALIGN
SPAN = STEP + ALIGN
far_below = -1e30


def static_tables(image_count):
    rows = np.arange(WIN_COUNT * SLOT)
    win, place = rows // SLOT, rows % SLOT
    row = (win // (GRID // WIN) * WIN + place // WIN + SHIFT) % GRID
    col = (win % (GRID // WIN) * WIN + place % WIN + SHIFT) % GRID
    token = np.where(place < WIN * WIN, row * GRID + col, -1)
    offset = np.arange(image_count) * (IMAGE - STEP)
    column = np.where(token[None] >= 0, token[None] + offset[:, None], -1)
    places = np.arange(SLOT)
    live = places < WIN * WIN
    pr, pc = places // WIN, places % WIN
    rel = (pr[None, :] - pr[:, None] + WIN - 1) * (2 * WIN - 1) + pc[None, :] - pc[:, None] + WIN - 1
    rel = np.where(live[:, None] & live[None, :], rel, -1)
    cells = np.arange(GRID)
    region = np.where(cells < GRID - WIN, 0, np.where(cells < GRID - SHIFT, 1, 2))
    shifted_row = (win // (GRID // WIN) * WIN + np.minimum(place // WIN, WIN - 1)).reshape(WIN_COUNT, SLOT)
    shifted_col = (win % (GRID // WIN) * WIN + place % WIN).reshape(WIN_COUNT, SLOT)
    ids = region[shifted_row] * 3 + region[shifted_col]
    mask = np.where(ids[:, :, None] == ids[:, None, :], 0.0, mask_value)
    mask = np.where(live[None, None, :] & live[None, :, None], mask, 0.0)
    mask = np.where(live[None, :, None], mask, far_below)
    return column.astype(np.int32), rel.astype(np.int32), mask.astype(np.float32)


def attention_tables(rel_table, image_count):
    column, rel, mask = static_tables(image_count)
    spots = np.arange(SPAN, dtype=np.int32)
    perm = jnp.asarray((column[:, :, None] == spots).astype(np.float32)).astype(jnp.bfloat16)
    perm_t = jnp.asarray((column[:, None, :] == spots[:, None]).astype(np.float32)).astype(jnp.bfloat16)
    heads = rel_table.shape[0]
    onehot = (jnp.arange(RELS, dtype=jnp.int32)[:, None] == jnp.asarray(rel.reshape(1, -1))).astype(
        jnp.bfloat16
    )
    bias = lax.dot_general(
        rel_table, onehot, (((1,), (0,)), ((), ())), preferred_element_type=jnp.float32
    )
    bias = bias.reshape(heads // PACK, PACK, SLOT, SLOT).transpose(0, 2, 1, 3)
    bias = bias[None] + jnp.asarray(mask)[:, None, :, None, :]
    bias = bias.reshape(WIN_COUNT, heads // PACK, SLOT, PACK * SLOT)
    owner = np.arange(PACK * SLOT)[:, None] // SLOT == np.arange(PACK * HD)[None, :] // HD
    owner = jnp.asarray(owner.astype(np.float32)).astype(jnp.bfloat16)
    return perm, perm_t, bias, owner, onehot


def spread(rows, owner):
    return jnp.concatenate([rows] * PACK, axis=0) * owner


def gather_heads(full):
    lanes = lax.broadcasted_iota(jnp.int32, (SLOT, PACK * HD), 1) // HD
    total = full[:SLOT]
    for h in range(1, PACK):
        total = jnp.where(lanes == h, full[h * SLOT : (h + 1) * SLOT], total)
    return total


def forward_kernel(qkv_ref, perm_ref, perm_t_ref, bias_ref, owner_ref, context_ref, windows_ref, probs_ref, ctx_ref):
    image = pl.program_id(0)
    width = context_ref.shape[1]
    groups = width // (PACK * HD)
    start = pl.multiple_of(image * STEP, ALIGN)
    windows_ref[0] = matmul(perm_ref[0], qkv_ref[pl.ds(start, SPAN), :]).astype(jnp.bfloat16)
    for w in range(WIN_COUNT):
        rows = slice(w * SLOT, (w + 1) * SLOT)
        for g in range(groups):
            low = g * PACK * HD
            query = windows_ref[0, rows, low : low + PACK * HD]
            keys = windows_ref[0, rows, width + low : width + low + PACK * HD]
            values = windows_ref[0, rows, 2 * width + low : 2 * width + low + PACK * HD]
            scores = matmul_nt(keys, spread(query, owner_ref[...])) * HD ** (-0.5) + bias_ref[w, g]
            raised = jnp.exp(scores - jnp.max(scores, 0, keepdims=True))
            probs = raised * (1.0 / jnp.sum(raised, 0, keepdims=True))
            probs_ref[0, w * groups + g] = probs
            full = matmul_tn(probs.astype(jnp.bfloat16), values)
            ctx_ref[rows, low : low + PACK * HD] = gather_heads(full).astype(jnp.bfloat16)

    @pl.when(image == 0)
    def _():
        context_ref[...] = jnp.zeros_like(context_ref)

    context_ref[pl.ds(start, SPAN), :] += matmul(perm_t_ref[0], ctx_ref[...]).astype(jnp.bfloat16)


def backward_kernel(
    d_context_ref, windows_ref, probs_ref, perm_ref, perm_t_ref, owner_ref,
    d_mixed_ref, d_bias_ref, d_qv_ref, d_ctx_ref, d_win_ref,
):
    image = pl.program_id(0)
    width = d_context_ref.shape[1]
    groups = width // (PACK * HD)
    start = pl.multiple_of(image * STEP, ALIGN)

    @pl.when(image == 0)
    def _():
        d_mixed_ref[...] = jnp.zeros_like(d_mixed_ref)
        d_bias_ref[...] = jnp.zeros_like(d_bias_ref)
        d_qv_ref[...] = jnp.zeros_like(d_qv_ref)

    d_ctx_ref[...] = matmul(perm_ref[0], d_context_ref[pl.ds(start, SPAN), :]).astype(jnp.bfloat16)
    for g in range(groups):
        low = g * PACK * HD
        cols = slice(low, low + PACK * HD)
        d_bias = jnp.zeros((SLOT, PACK * SLOT), jnp.float32)
        d_query_sum = jnp.zeros((1, PACK * HD), jnp.float32)
        d_value_sum = jnp.zeros((1, PACK * HD), jnp.float32)
        for w in range(WIN_COUNT):
            rows = slice(w * SLOT, (w + 1) * SLOT)
            query = windows_ref[0, rows, low : low + PACK * HD]
            keys = windows_ref[0, rows, width + low : width + low + PACK * HD]
            values = windows_ref[0, rows, 2 * width + low : 2 * width + low + PACK * HD]
            probs = probs_ref[0, w * groups + g]
            d_wide = spread(d_ctx_ref[rows, cols], owner_ref[...])
            d_probs = matmul_nt(values, d_wide)
            d_values = matmul(probs.astype(jnp.bfloat16), d_wide)
            d_scores = probs * (d_probs - jnp.sum(probs * d_probs, 0, keepdims=True))
            d_bias = d_bias + d_scores
            d_low = d_scores.astype(jnp.bfloat16)
            d_keys = matmul(d_low, spread(query, owner_ref[...])) * HD ** (-0.5)
            d_query = gather_heads(matmul_tn(d_low, keys)) * HD ** (-0.5)
            d_win_ref[rows, low : low + PACK * HD] = d_query.astype(jnp.bfloat16)
            d_win_ref[rows, width + low : width + low + PACK * HD] = d_keys.astype(jnp.bfloat16)
            d_win_ref[rows, 2 * width + low : 2 * width + low + PACK * HD] = d_values.astype(jnp.bfloat16)
            d_query_sum = d_query_sum + jnp.sum(d_query, 0, keepdims=True)
            d_value_sum = d_value_sum + jnp.sum(d_values, 0, keepdims=True)
        d_bias_ref[g] += d_bias
        d_qv_ref[0:1, cols] += d_query_sum
        d_qv_ref[1:2, cols] += d_value_sum
    d_mixed_ref[pl.ds(start, SPAN), :] += matmul(perm_t_ref[0], d_win_ref[...]).astype(jnp.bfloat16)


def whole(shape):
    return pl.BlockSpec(shape, lambda n: (0,) * len(shape))


def per_image(shape):
    return pl.BlockSpec((1,) + shape, lambda n: (n,) + (0,) * len(shape))


def attend_forward(qkv, tables, later):
    perm, perm_t, bias, owner, _ = tables
    tok, wide = qkv.shape
    width = wide // 3
    count, spots = perm.shape[:2]
    tiles = WIN_COUNT * width // (PACK * HD)
    sizes = mesh_sizes()
    copies = len(later) * (sizes[0] - 1)
    return pl.pallas_call(
        functools.partial(forward_stage, sizes),
        grid=(count,),
        in_specs=[whole(qkv.shape), per_image((spots, SPAN)), per_image((SPAN, spots)), whole(bias.shape), whole(owner.shape)]
        + [whole(rows.shape) for rows in later],
        out_specs=[whole((tok, width)), per_image((spots, wide)), per_image((tiles, SLOT, PACK * SLOT))] + [hbm_spec()] * len(later),
        out_shape=[
            jax.ShapeDtypeStruct((tok, width), jnp.bfloat16),
            jax.ShapeDtypeStruct((count, spots, wide), jnp.bfloat16),
            jax.ShapeDtypeStruct((count, tiles, SLOT, PACK * SLOT), jnp.float32),
        ]
        + [jax.ShapeDtypeStruct((rows.shape[0] * sizes[0], rows.shape[1]), rows.dtype) for rows in later],
        scratch_shapes=[
            pltpu.VMEM((spots, width), jnp.bfloat16),
            pltpu.SemaphoreType.DMA((copies,)),
            pltpu.SemaphoreType.DMA((copies,)),
            pltpu.SemaphoreType.DMA((len(later),)),
        ],
        compiler_params=pltpu.CompilerParams(collective_id=2, has_side_effects=True, vmem_limit_bytes=32 << 20),
        cost_estimate=pl.CostEstimate(flops=6_000_000_000, bytes_accessed=24_000_000, transcendentals=tok * width * 2),
        name="attend_forward",
    )(qkv, perm, perm_t, bias, owner, *later)


def attend_backward(d_context, windows, probs, tables, sums):
    perm, perm_t, _, owner, onehot = tables
    tok, width = d_context.shape
    count, spots, wide = windows.shape
    groups = width // (PACK * HD)
    tiles = probs.shape[1]
    sizes = mesh_sizes()
    blocks = [(full.shape[0] // sizes[0], full.shape[1]) for full in sums]
    halves = [
        pltpu.VMEM((sizes[0] >> (bit + 1),) + block, jnp.bfloat16) for block in blocks for bit in range(bits_of(sizes[0]))
    ]
    copies = len(sums) * (sizes[0] - 1)
    d_mixed, d_bias, d_qv, *sums = pl.pallas_call(
        functools.partial(backward_stage, sizes),
        grid=(count,),
        in_specs=[
            whole(d_context.shape), per_image((spots, wide)), per_image((tiles, SLOT, PACK * SLOT)),
            per_image((spots, SPAN)), per_image((SPAN, spots)), whole(owner.shape),
        ]
        + [whole(full.shape) for full in sums],
        out_specs=[whole((tok, wide)), whole((groups, SLOT, PACK * SLOT)), whole((2, width))] + [whole(block) for block in blocks],
        out_shape=[
            jax.ShapeDtypeStruct((tok, wide), jnp.bfloat16),
            jax.ShapeDtypeStruct((groups, SLOT, PACK * SLOT), jnp.float32),
            jax.ShapeDtypeStruct((2, width), jnp.float32),
        ]
        + [jax.ShapeDtypeStruct(block, jnp.bfloat16) for block in blocks],
        scratch_shapes=[pltpu.VMEM((spots, width), jnp.bfloat16), pltpu.VMEM((spots, wide), jnp.bfloat16)]
        + halves
        + [pltpu.SemaphoreType.DMA((copies,)), pltpu.SemaphoreType.DMA((copies,))],
        compiler_params=pltpu.CompilerParams(collective_id=3, has_side_effects=True, vmem_limit_bytes=44 << 20),
        cost_estimate=pl.CostEstimate(flops=9_000_000_000, bytes_accessed=32_000_000, transcendentals=0),
        name="attend_backward",
    )(d_context, windows, probs, perm, perm_t, owner, *sums)
    d_bias = d_bias.reshape(groups, SLOT, PACK, SLOT).transpose(0, 2, 1, 3).reshape(groups * PACK, SLOT * SLOT)
    d_table = lax.dot_general(
        onehot.astype(jnp.float32), d_bias, (((1,), (1,)), ((), ())), precision=lax.Precision.HIGHEST
    )
    return d_mixed, d_qv, d_table, sums


def gelu_parts(pre_act):
    cdf_part = 0.5 * (1.0 + jax.scipy.special.erf(pre_act * inv_root_two))
    return (
        pre_act * cdf_part,
        cdf_part + pre_act * jnp.exp(-0.5 * pre_act * pre_act) * inv_root_two_pi,
    )


def layer_norm(rows, gain, shift):
    row_mean = jnp.mean(rows, -1, keepdims=True)
    row_var = jnp.mean(rows * rows, -1, keepdims=True) - row_mean * row_mean
    inv_std = lax.rsqrt(row_var + eps_norm)
    normed = (rows - row_mean) * inv_std
    return (normed, inv_std, normed * gain + shift)


def norm_back(d_out, normed, inv_std, gain):
    d_normed = d_out * gain
    return inv_std * (
        d_normed
        - jnp.mean(d_normed, -1, keepdims=True)
        - normed * jnp.mean(d_normed * normed, -1, keepdims=True)
    )


ROW_PAD = 16


def bit_of(index, bit):
    return (index // (1 << bit)) % 2


def bits_of(size):
    return size.bit_length() - 1


def greet(gx_size, gy_size):
    mine, row = lax.axis_index("gx"), lax.axis_index("gy")
    barrier = pltpu.get_barrier_semaphore()
    for name, index, size in (("gx", mine, gx_size), ("gy", row, gy_size)):
        for bit in range(bits_of(size)):
            there = index + (1 << bit) * (1 - 2 * bit_of(index, bit))
            pl.semaphore_signal(barrier, inc=1, device_id={name: there}, device_id_type=pl.DeviceIdType.MESH)
    pl.semaphore_wait(barrier, bits_of(gx_size) + bits_of(gy_size))


class Sender:
    def __init__(self, send, recv):
        self.send, self.recv, self.used = send, recv, 0

    def plan(self, src, dst, name, there):
        copy = pltpu.make_async_remote_copy(
            src_ref=src,
            dst_ref=dst,
            send_sem=self.send.at[self.used],
            recv_sem=self.recv.at[self.used],
            device_id={name: there},
            device_id_type=pl.DeviceIdType.MESH,
        )
        self.used += 1
        return copy


def phase(waits=(), act=None, starts=()):
    def run():
        for copy in waits:
            copy.wait()
        if act is not None:
            act()
        for copy in starts:
            copy.start()

    return run


def split_steps(index, size):
    top = bits_of(size) - 1
    core = index % 2
    high, low = bit_of(index, top), bit_of(index, top - 1)
    big, small = 1 << top, 1 << (top - 1)
    first_step = (1 - core) * big * (1 - 2 * high) + core * small * (1 - 2 * low)
    second_step = (1 - core) * small * (1 - 2 * low) + core * big * (1 - 2 * high)
    return core, high, low, first_step, second_step


def gather_column(sender, local, slots, sem, sizes, act=None):
    row = lax.axis_index("gy")
    own = [pltpu.make_async_copy(ref, slot.at[row], sem.at[n]) for n, (ref, slot) in enumerate(zip(local, slots))]
    waits, starts, phases = [], list(own), []
    held = [row]
    for bit in range(bits_of(sizes[1]))[::-1]:
        step = (1 << bit) * (1 - 2 * bit_of(row, bit))
        copies = [
            sender.plan(local[n] if place == 0 else slot.at[at], slot.at[at], "gy", row + step)
            for place, at in enumerate(held)
            for n, slot in enumerate(slots)
        ]
        phases.append(phase(waits, None, starts + copies))
        waits, starts = copies, []
        held = held + [at + step for at in held]
    phases.append(phase(waits + own, act))
    return phases


def join_rows(slots, rows_ref, groups):
    gy_size, _, wide = slots.shape
    width = wide // groups
    for i in range(gy_size):
        for k in range(groups):
            low = (k * gy_size + i) * width
            rows_ref[:, low : low + width] = slots[i, :, k * width : (k + 1) * width]


def gather_plane(sender, own, full, sem, sizes):
    gx_size = sizes[0]
    mine = lax.axis_index("gx")
    rows = own.shape[0]
    core, _, _, first_step, second_step = split_steps(mine, gx_size)
    steps = [first_step, second_step]
    for bit in range(1, bits_of(gx_size) - 2)[::-1]:
        steps.append((1 << bit) * (1 - 2 * bit_of(mine, bit)))
    over = 1 - 2 * core

    def view(at):
        return full.at[pl.ds(pl.multiple_of(at * rows, rows), rows), :]

    def push(at, first, there):
        return sender.plan(own if first else view(at), view(at), "gx", there)

    keep = pltpu.make_async_copy(own, view(mine), sem)
    held, fresh = [mine], [mine]
    waits, shared, phases = [], [keep], []
    for place, step in enumerate(steps):
        copies = [push(at, n == 0, mine + step) for n, at in enumerate(held)]
        across = [push(at, place == 0, mine + over) for at in fresh]
        phases.append(phase(waits, None, copies + across + ([keep] if place == 0 else [])))
        waits = copies
        shared += across
        fresh = [at + step for at in held]
        held = held + fresh
    across = [push(at, False, mine + over) for at in fresh]
    phases.append(phase(waits, None, across))
    phases.append(phase(shared + across))
    return phases


def add_into(target, left, right):
    target[...] = (left[...].astype(jnp.float32) + right[...].astype(jnp.float32)).astype(target.dtype)


def add_arrived(copies, came, kept, out=None):
    def run():
        for k, (copy, view) in enumerate(zip(copies, kept)):
            copy.wait()
            add_into(came.at[k] if out is None else out, came.at[k], view)

    return run


def share_plane(sender, full, halves, out, sizes):
    gx_size = sizes[0]
    mine = lax.axis_index("gx")
    rows = full.shape[0] // gx_size
    core, high, low, first_step, second_step = split_steps(mine, gx_size)

    def block(at):
        return full.at[pl.ds(pl.multiple_of(at * rows, rows), rows), :]

    held, act, phases = block, None, []
    count = gx_size
    for bit in range(bits_of(gx_size)):
        came = halves[bit]
        count //= 2
        own = bit_of(mine, bit)
        if count >= 4:
            step = (1 << bit) * (1 - 2 * own)
            away = [2 * k + 1 - own for k in range(count)]
            kept = [2 * k + own for k in range(count)]
        elif count == 2:
            step = second_step
            away = [(1 - core) * (2 * k + 1 - low) + core * (2 * (1 - high) + k) for k in range(count)]
            kept = [(1 - core) * (2 * k + low) + core * (2 * high + k) for k in range(count)]
        else:
            step = first_step
            last = (1 - core) * high + core * low
            away, kept = [1 - last], [last]
        copies = [sender.plan(held(at), came.at[k], "gx", mine + step) for k, at in enumerate(away)]
        phases.append(phase((), act, copies))
        act = add_arrived(copies, came, [held(at) for at in kept], out if count == 1 else None)
        held = (lambda ref: lambda at: ref.at[at])(came)
    phases.append(phase((), act))
    return phases


def share_column(sender, total, slots, halves, out, groups, sizes):
    gy_size = sizes[1]
    row = lax.axis_index("gy")
    width = slots.shape[2] // groups

    def act():
        for i in range(gy_size):
            for k in range(groups):
                low = (k * gy_size + i) * width
                slots[i, :, k * width : (k + 1) * width] = total[:, low : low + width]

    held, phases = slots, []
    count = gy_size
    for bit in range(bits_of(gy_size)):
        came = halves[bit]
        count //= 2
        own = bit_of(row, bit)
        step = (1 << bit) * (1 - 2 * own)
        copies = [sender.plan(held.at[2 * k + 1 - own], came.at[k], "gy", row + step) for k in range(count)]
        phases.append(phase((), act, copies))
        act = add_arrived(copies, came, [held.at[2 * k + own] for k in range(count)], out if count == 1 else None)
        held = came
    phases.append(phase((), act))
    return phases


def sum_small(sender, value, came, totals, out, sizes):
    held, act, phases = value, None, []
    stage = 0
    stages = bits_of(sizes[0]) + bits_of(sizes[1])
    for name, size in (("gx", sizes[0]), ("gy", sizes[1])):
        index = lax.axis_index(name)
        for bit in range(bits_of(size)):
            there = index + (1 << bit) * (1 - 2 * bit_of(index, bit))
            copy = sender.plan(held, came.at[stage], name, there)
            phases.append(phase((), act, [copy]))
            target = out if stage == stages - 1 else totals.at[stage]
            act = add_small(copy, held, came, stage, target)
            held = target
            stage += 1
    phases.append(phase((), act))
    return phases


def add_small(copy, held, came, stage, target):
    def run():
        copy.wait()
        target[...] = held[...] + came[stage]

    return run


def gather_kernel(sizes, qkv_ref, small_ref, proj_ref, fc1_ref, fc2_ref, qkv_full, small_all, proj_rows, fc1_rows, fc2_rows,
                  qkv_slots, proj_slots, fc1_slots, fc2_slots, qkv_rows, send, recv, own_sem, keep_sem):
    greet(*sizes)
    sender = Sender(send, recv)

    def join_later():
        join_rows(proj_slots, proj_rows, 1)
        join_rows(fc1_slots, fc1_rows, 1)
        join_rows(fc2_slots, fc2_rows, 1)

    first = gather_column(
        sender, [qkv_ref, small_ref], [qkv_slots, small_all], own_sem.at[0], sizes, lambda: join_rows(qkv_slots, qkv_rows, 3)
    )
    second = gather_column(
        sender, [proj_ref, fc1_ref, fc2_ref], [proj_slots, fc1_slots, fc2_slots], own_sem.at[1], sizes, join_later
    )
    plane = gather_plane(sender, qkv_rows, qkv_full, keep_sem.at[0], sizes)
    for run in first:
        run()
    while plane or second:
        for queue in (plane, second):
            if queue:
                queue.pop(0)()


def vmem_spec():
    return pl.BlockSpec(memory_space=pltpu.VMEM)


def hbm_spec():
    return pl.BlockSpec(memory_space=pl.ANY)


def mesh_sizes():
    return lax.axis_size("gx"), lax.axis_size("gy")


def gather_weights(qkv, small, proj_t, fc1, fc2_t):
    sizes = mesh_sizes()
    gx_size, gy_size = sizes
    rows = qkv.shape[0]
    later = [jax.ShapeDtypeStruct((rows, v.shape[1] * gy_size), v.dtype) for v in (proj_t, fc1, fc2_t)]
    wide = qkv.shape[1] * gy_size
    count = 5 * (gy_size - 1) + gx_size - 1
    return pl.pallas_call(
        functools.partial(gather_kernel, sizes),
        in_specs=[vmem_spec()] * 5,
        out_specs=[hbm_spec()] + [vmem_spec()] * 4,
        out_shape=[jax.ShapeDtypeStruct((rows * gx_size, wide), qkv.dtype), jax.ShapeDtypeStruct((gy_size,) + small.shape, small.dtype)]
        + later,
        scratch_shapes=[pltpu.VMEM((gy_size,) + v.shape, v.dtype) for v in (qkv, proj_t, fc1, fc2_t)]
        + [
            pltpu.VMEM((rows, wide), qkv.dtype),
            pltpu.SemaphoreType.DMA((count,)), pltpu.SemaphoreType.DMA((count,)), pltpu.SemaphoreType.DMA((2, 3)),
            pltpu.SemaphoreType.DMA((1,)),
        ],
        compiler_params=pltpu.CompilerParams(collective_id=0, has_side_effects=True, vmem_limit_bytes=16 << 20),
        name="gather_weights",
    )(qkv, small, proj_t, fc1, fc2_t)


def share_kernel(sizes, groups, whole_count, *refs):
    gx_bits, gy_bits = bits_of(sizes[0]), bits_of(sizes[1])
    arrays = len(groups)
    refs = list(refs)

    def take(count):
        out = refs[:count]
        del refs[:count]
        return out

    inputs, (small,) = take(arrays), take(1)
    outs, (small_out,) = take(arrays), take(1)
    planes = [take(gx_bits) for _ in range(whole_count)]
    totals = take(whole_count)
    slots = take(arrays)
    columns = [take(gy_bits) for _ in range(arrays)]
    small_came, small_totals, send, recv = take(4)
    greet(*sizes)
    sender = Sender(send, recv)
    streams = []
    for n in range(arrays):
        phases = share_plane(sender, inputs[n], planes[n], totals[n], sizes) if n < whole_count else []
        total = totals[n] if n < whole_count else inputs[n]
        phases += share_column(sender, total, slots[n], columns[n], outs[n], groups[n], sizes)
        streams.append(phases)
    streams.append(sum_small(sender, small, small_came, small_totals, small_out, sizes))
    while any(streams):
        for queue in streams:
            if queue:
                queue.pop(0)()


def share_sums(fulls, rows_sums, groups, small):
    sizes = mesh_sizes()
    gx_size, gy_size = sizes
    gx_bits, gy_bits = bits_of(gx_size), bits_of(gy_size)
    rows = fulls[0].shape[0] // gx_size
    arrays = tuple(fulls) + tuple(rows_sums)
    planes, slots, columns = [], [], []
    for full in fulls:
        planes += [pltpu.VMEM((gx_size >> (bit + 1), rows, full.shape[1]), full.dtype) for bit in range(gx_bits)]
    for value in arrays:
        wide = value.shape[1] // gy_size
        slots.append(pltpu.VMEM((gy_size, rows, wide), value.dtype))
        columns += [pltpu.VMEM((gy_size >> (bit + 1), rows, wide), value.dtype) for bit in range(gy_bits)]
    stages = gx_bits + gy_bits
    count = len(fulls) * (gx_size - 1) + len(arrays) * (gy_size - 1) + stages
    return pl.pallas_call(
        functools.partial(share_kernel, sizes, groups, len(fulls)),
        in_specs=[vmem_spec()] * (len(arrays) + 1),
        out_specs=[vmem_spec()] * (len(arrays) + 1),
        out_shape=[jax.ShapeDtypeStruct((rows, value.shape[1] // gy_size), jnp.float32) for value in arrays]
        + [jax.ShapeDtypeStruct(small.shape, small.dtype)],
        scratch_shapes=planes + [pltpu.VMEM((rows, full.shape[1]), full.dtype) for full in fulls] + slots + columns + [
            pltpu.VMEM((stages,) + small.shape, small.dtype),
            pltpu.VMEM((stages,) + small.shape, small.dtype),
            pltpu.SemaphoreType.DMA((count,)),
            pltpu.SemaphoreType.DMA((count,)),
        ],
        compiler_params=pltpu.CompilerParams(collective_id=1, has_side_effects=True, vmem_limit_bytes=24 << 20),
        name="share_sums",
    )(*arrays, small)


def forward_stage(
    sizes, qkv_ref, perm_ref, perm_t_ref, bias_ref, owner_ref, proj_rows, fc1_rows, fc2_rows,
    context_ref, windows_ref, probs_ref, proj_full, fc1_full, fc2_full, ctx_ref, send, recv, keep_sem,
):
    image, last = pl.program_id(0), pl.num_programs(0) - 1

    @pl.when(image == 0)
    def _():
        greet(*sizes)

    sender = Sender(send, recv)
    own = (proj_rows, fc1_rows, fc2_rows)
    fulls = (proj_full, fc1_full, fc2_full)
    streams = [gather_plane(sender, own[n], fulls[n], keep_sem.at[n], sizes) for n in range(3)]

    @pl.when(image == 0)
    def _():
        for phases in streams:
            phases[0]()

    for n, phases in enumerate(streams):
        @pl.when(image == jnp.minimum(n + 1, last))
        def _():
            phases[1]()

    forward_kernel(
        qkv_ref, perm_ref, perm_t_ref, bias_ref, owner_ref, context_ref, windows_ref, probs_ref, ctx_ref
    )

    @pl.when(image == last)
    def _():
        for place in range(2, len(streams[0])):
            for phases in streams:
                phases[place]()


def backward_stage(
    sizes, d_context_ref, windows_ref, probs_ref, perm_ref, perm_t_ref, owner_ref, d_fc1_ref, d_fc2_ref,
    d_mixed_ref, d_bias_ref, d_qv_ref, fc1_sum, fc2_sum, d_ctx_ref, d_win_ref, *rest,
):
    image, last = pl.program_id(0), pl.num_programs(0) - 1
    gx_bits = bits_of(sizes[0])
    fc1_halves, fc2_halves, (send, recv) = rest[:gx_bits], rest[gx_bits : 2 * gx_bits], rest[2 * gx_bits :]

    @pl.when(image == 0)
    def _():
        greet(*sizes)

    sender = Sender(send, recv)
    streams = [
        share_plane(sender, d_fc1_ref, fc1_halves, fc1_sum, sizes),
        share_plane(sender, d_fc2_ref, fc2_halves, fc2_sum, sizes),
    ]

    @pl.when(image == 0)
    def _():
        for phases in streams:
            phases[0]()

    @pl.when(image == jnp.minimum(1, last))
    def _():
        for phases in streams:
            phases[1]()

    @pl.when(image == last)
    def _():
        streams[0][2]()

    backward_kernel(
        d_context_ref, windows_ref, probs_ref, perm_ref, perm_t_ref, owner_ref,
        d_mixed_ref, d_bias_ref, d_qv_ref, d_ctx_ref, d_win_ref,
    )

    @pl.when(image == last)
    def _():
        streams[1][2]()
        for place in range(3, len(streams[0])):
            for phases in streams:
                phases[place]()


def pack_rows(values):
    rows = []
    for value in values:
        flat = value.reshape(-1)
        rows.append(jnp.pad(flat, (0, -flat.shape[0] % 1024)).reshape(-1, 128))
    return jnp.concatenate(rows, 0)


def unpack_rows(packed, shapes):
    at, out = 0, []
    for shape in shapes:
        size = int(np.prod(shape))
        count = (size + 1023) // 1024 * 8
        out.append(packed[at : at + count].reshape(-1)[:size].reshape(shape))
        at += count
    return out


def own_columns(summed, axis):
    size = summed.shape[axis] // lax.axis_size("gy")
    return lax.dynamic_slice_in_dim(summed, lax.axis_index("gy") * size, size, axis)


def local_live(tok_local, live_images):
    position = lax.axis_index("gy")
    per_device = tok_local // (GRID * GRID)
    slot_index = position * per_device + jnp.arange(tok_local, dtype=jnp.int32) // (GRID * GRID)
    return slot_index < live_images[0]


def blocked_layer(block_input, cotangent, live_images, params):
    (
        ln1_gain,
        ln1_bias,
        qkv_weight,
        qv_bias,
        rel_table,
        proj_weight,
        proj_bias,
        ln2_gain,
        ln2_bias,
        fc1_weight,
        fc1_bias,
        fc2_weight,
        fc2_bias,
    ) = params
    tok_local, width = block_input.shape
    block_rows = qkv_weight.shape[0]
    part, hidden_local = qkv_weight.shape[2], fc1_weight.shape[1]
    heads_local = rel_table.shape[1]

    def lane_row(value):
        value = value.reshape(value.shape[0], -1)
        return jnp.pad(value, ((0, 0), (0, hidden_local - value.shape[1])))

    small = jnp.concatenate([fc1_bias[None], lane_row(qv_bias.reshape(1, -1)), lane_row(rel_table.T)], 0)
    small = jnp.pad(small, ((0, ROW_PAD - small.shape[0]), (0, 0)))
    qkv_flat, small, *later = gather_weights(
        qkv_weight.reshape(block_rows, -1), small, proj_weight.T, fc1_weight, fc2_weight.T
    )
    fc1_bias = small[:, 0].reshape(-1)
    qv_bias = small[:, 1, : 2 * part].reshape(-1, 2, part).transpose(1, 0, 2).reshape(2, -1)
    rel_table = small[:, 2 : 2 + heads_local, :RELS].reshape(-1, RELS)
    gain_one = ln1_gain.astype(jnp.float32)
    gain_two = ln2_gain.astype(jnp.float32)
    resid = block_input.astype(jnp.float32)
    normed_one, scale_one, pre_one = layer_norm(resid, gain_one, ln1_bias.astype(jnp.float32))
    hidden_one = (pre_one.astype(jnp.bfloat16))
    bias_row = jnp.stack([qv_bias[0], jnp.zeros_like(qv_bias[0]), qv_bias[1]]).reshape(1, 3 * width)
    mixed = (matmul(hidden_one, qkv_flat) + bias_row.astype(jnp.float32)).astype(jnp.bfloat16)
    tables = attention_tables(rel_table, tok_local // IMAGE)
    context, windows, probs, proj_cols, fc1_rows, fc2_cols = attend_forward(mixed, tables, later)
    resid_one = resid + (matmul_nt(context, proj_cols)) + proj_bias.astype(jnp.float32)
    normed_two, scale_two, pre_two = layer_norm(resid_one, gain_two, ln2_bias.astype(jnp.float32))
    hidden_two = (pre_two.astype(jnp.bfloat16))
    pre_act = matmul(hidden_two, fc1_rows) + fc1_bias.astype(jnp.float32)
    act_full, slope = gelu_parts(pre_act)
    act_low = act_full.astype(jnp.bfloat16)
    output = (
        resid_one + (matmul_nt(act_low, fc2_cols)) + fc2_bias.astype(jnp.float32)
    ).astype(jnp.bfloat16)
    live_rows = local_live(tok_local, live_images)
    grad_out = jnp.where(live_rows[:, None], cotangent, jnp.zeros_like(cotangent))
    grad_float = grad_out.astype(jnp.float32)
    grad_full = (grad_out)
    d_fc2_bias = jnp.sum(grad_float, 0)
    d_fc2_weight = matmul_tn(grad_full, act_low).astype(jnp.bfloat16)
    d_pre = matmul(grad_full, fc2_cols) * slope
    d_fc1_bias = jnp.sum(d_pre, 0)
    d_pre_low = d_pre.astype(jnp.bfloat16)
    d_fc1_weight = matmul_tn(hidden_two, d_pre_low).astype(jnp.bfloat16)
    d_hidden_two = (matmul_nt(d_pre_low, fc1_rows))
    d_ln2_gain = jnp.sum(d_hidden_two * normed_two, 0)
    d_ln2_bias = jnp.sum(d_hidden_two, 0)
    d_resid_one = grad_float + norm_back(d_hidden_two, normed_two, scale_two, gain_two)
    d_proj_bias = jnp.sum(d_resid_one, 0)
    d_resid_full = (d_resid_one.astype(jnp.bfloat16))
    d_proj_weight = matmul_tn(d_resid_full, context).astype(jnp.bfloat16)
    d_context = matmul(d_resid_full, proj_cols).astype(jnp.bfloat16)
    d_mixed, d_qv_bias, d_table, sums = attend_backward(d_context, windows, probs, tables, (d_fc1_weight, d_fc2_weight))
    d_qkv_weight = matmul_tn(hidden_one, d_mixed).astype(jnp.bfloat16)
    d_hidden_one = (matmul_nt(d_mixed, qkv_flat))
    d_ln1_gain = jnp.sum(d_hidden_one * normed_one, 0)
    d_ln1_bias = jnp.sum(d_hidden_one, 0)
    d_input = (d_resid_one + norm_back(d_hidden_one, normed_one, scale_one, gain_one)).astype(
        jnp.bfloat16
    )
    own = (d_ln1_gain, d_ln1_bias, d_proj_bias, d_ln2_gain, d_ln2_bias, d_fc2_bias, d_qv_bias, d_table, d_fc1_bias)
    d_qkv_weight, d_proj_weight, d_fc1_weight, d_fc2_weight, sums = share_sums(
        (d_qkv_weight, d_proj_weight), sums, (3, 1, 1, 1), pack_rows(own)
    )
    d_fc2_weight = d_fc2_weight.T
    d_proj_weight = d_proj_weight.T
    d_qkv_weight = d_qkv_weight.reshape(block_rows, 3, part)
    sums = unpack_rows(sums, [value.shape for value in own])
    norm_sums = sums[:6]
    head_sums = (own_columns(sums[6], 1), own_columns(sums[7], 1), own_columns(sums[8], 0))
    return (
        output,
        d_input,
        norm_sums[0],
        norm_sums[1],
        d_qkv_weight,
        head_sums[0],
        head_sums[1],
        d_proj_weight,
        norm_sums[2],
        norm_sums[3],
        norm_sums[4],
        d_fc1_weight,
        head_sums[2],
        d_fc2_weight,
        norm_sums[5],
    )


def shards(
    block_input,
    cotangent,
    live_images,
    ln1_gain,
    ln1_bias,
    qkv_weight,
    qv_bias,
    rel_table,
    proj_weight,
    proj_bias,
    ln2_gain,
    ln2_bias,
    fc1_weight,
    fc1_bias,
    fc2_weight,
    fc2_bias,
):
    params = (
        ln1_gain,
        ln1_bias,
        qkv_weight,
        qv_bias,
        rel_table,
        proj_weight,
        proj_bias,
        ln2_gain,
        ln2_bias,
        fc1_weight,
        fc1_bias,
        fc2_weight,
        fc2_bias,
    )
    return blocked_layer(block_input, cotangent, live_images, params)


def solution(mesh):
    return jax.shard_map(
        shards,
        mesh=mesh,
        in_specs=(
            P(("gx", "gy"), None),
            P(("gx", "gy"), None),
            P("gx"),
            P(),
            P(),
            P("gx", None, "gy"),
            P(None, "gy"),
            P(None, "gy"),
            P("gy", "gx"),
            P(),
            P(),
            P(),
            P("gx", "gy"),
            P("gy"),
            P("gy", "gx"),
            P(),
        ),
        out_specs=(
            P(("gx", "gy"), None),
            P(("gx", "gy"), None),
            P(),
            P(),
            P("gx", None, "gy"),
            P(None, "gy"),
            P(None, "gy"),
            P("gy", "gx"),
            P(),
            P(),
            P(),
            P("gx", "gy"),
            P("gy"),
            P("gy", "gx"),
            P(),
        ),
        check_vma=False,
    )
```

```python
import functools
import jax
import jax.numpy as jnp
from jax import lax
import numpy as np
from jax.experimental import pallas as pl
from jax.experimental.pallas import tpu as pltpu
from jax.sharding import PartitionSpec as P

HD = 32
GRID = 14
WIN = 7
SHIFT = 3
RELS = 169


eps_norm = 1e-05
mask_value = -100.0
inv_root_two = 0.7071067811865476
inv_root_two_pi = 0.3989422804014327


def matmul(left, right):
    return jnp.dot(left, right, preferred_element_type=jnp.float32)


def matmul_tn(left, right):
    return lax.dot_general(
        left, right, (((0,), (0,)), ((), ())), preferred_element_type=jnp.float32
    )


def matmul_nt(left, right):
    return lax.dot_general(
        left, right, (((1,), (1,)), ((), ())), preferred_element_type=jnp.float32
    )


SLOT = 64
PACK = 8
WIN_COUNT = (GRID // WIN) ** 2
IMAGE = GRID * GRID
ALIGN = 16
STEP = IMAGE // ALIGN * ALIGN
SPAN = STEP + ALIGN
far_below = -1e30


def static_tables(image_count):
    rows = np.arange(WIN_COUNT * SLOT)
    win, place = rows // SLOT, rows % SLOT
    row = (win // (GRID // WIN) * WIN + place // WIN + SHIFT) % GRID
    col = (win % (GRID // WIN) * WIN + place % WIN + SHIFT) % GRID
    token = np.where(place < WIN * WIN, row * GRID + col, -1)
    offset = np.arange(image_count) * (IMAGE - STEP)
    column = np.where(token[None] >= 0, token[None] + offset[:, None], -1)
    places = np.arange(SLOT)
    live = places < WIN * WIN
    pr, pc = places // WIN, places % WIN
    rel = (pr[None, :] - pr[:, None] + WIN - 1) * (2 * WIN - 1) + pc[None, :] - pc[:, None] + WIN - 1
    rel = np.where(live[:, None] & live[None, :], rel, -1)
    cells = np.arange(GRID)
    region = np.where(cells < GRID - WIN, 0, np.where(cells < GRID - SHIFT, 1, 2))
    shifted_row = (win // (GRID // WIN) * WIN + np.minimum(place // WIN, WIN - 1)).reshape(WIN_COUNT, SLOT)
    shifted_col = (win % (GRID // WIN) * WIN + place % WIN).reshape(WIN_COUNT, SLOT)
    ids = region[shifted_row] * 3 + region[shifted_col]
    mask = np.where(ids[:, :, None] == ids[:, None, :], 0.0, mask_value)
    mask = np.where(live[None, None, :] & live[None, :, None], mask, 0.0)
    mask = np.where(live[None, :, None], mask, far_below)
    return column.astype(np.int32), rel.astype(np.int32), mask.astype(np.float32)


def attention_tables(image_count):
    column, rel, _ = static_tables(image_count)
    spots = np.arange(SPAN, dtype=np.int32)
    perm = jnp.asarray((column[:, :, None] == spots).astype(np.float32)).astype(jnp.bfloat16)
    perm_t = jnp.asarray((column[:, None, :] == spots[:, None]).astype(np.float32)).astype(jnp.bfloat16)
    onehot = (jnp.arange(RELS, dtype=jnp.int32)[:, None] == jnp.asarray(rel.reshape(1, -1))).astype(jnp.bfloat16)
    owner = np.arange(PACK * SLOT)[:, None] // SLOT == np.arange(PACK * HD)[None, :] // HD
    owner = jnp.asarray(owner.astype(np.float32)).astype(jnp.bfloat16)
    return perm, perm_t, owner, onehot


def spread(rows, owner):
    return jnp.concatenate([rows] * PACK, axis=0) * owner


def gather_heads(full):
    lanes = lax.broadcasted_iota(jnp.int32, (SLOT, PACK * HD), 1) // HD
    total = full[:SLOT]
    for h in range(1, PACK):
        total = jnp.where(lanes == h, full[h * SLOT : (h + 1) * SLOT], total)
    return total


def forward_kernel(qkv_ref, perm_ref, perm_t_ref, bias_ref, owner_ref, context_ref, windows_ref, probs_ref, ctx_ref):
    image = pl.program_id(0)
    width = context_ref.shape[1]
    groups = width // (PACK * HD)
    start = pl.multiple_of(image * STEP, ALIGN)
    windows_ref[0] = matmul(perm_ref[0], qkv_ref[pl.ds(start, SPAN), :]).astype(jnp.bfloat16)
    for w in range(WIN_COUNT):
        rows = slice(w * SLOT, (w + 1) * SLOT)
        for g in range(groups):
            low = g * PACK * HD
            query = windows_ref[0, rows, low : low + PACK * HD]
            keys = windows_ref[0, rows, width + low : width + low + PACK * HD]
            values = windows_ref[0, rows, 2 * width + low : 2 * width + low + PACK * HD]
            scores = matmul_nt(keys, spread(query, owner_ref[...])) * HD ** (-0.5) + bias_ref[w, g]
            raised = jnp.exp(scores - jnp.max(scores, 0, keepdims=True))
            probs = raised * (1.0 / jnp.sum(raised, 0, keepdims=True))
            probs_ref[0, w * groups + g] = probs
            full = matmul_tn(probs.astype(jnp.bfloat16), values)
            ctx_ref[rows, low : low + PACK * HD] = gather_heads(full).astype(jnp.bfloat16)

    @pl.when(image == 0)
    def _():
        context_ref[...] = jnp.zeros_like(context_ref)

    context_ref[pl.ds(start, SPAN), :] += matmul(perm_t_ref[0], ctx_ref[...]).astype(jnp.bfloat16)


def backward_kernel(
    d_context_ref, windows_ref, probs_ref, perm_ref, perm_t_ref, owner_ref,
    d_mixed_ref, d_bias_ref, d_qv_ref, d_ctx_ref, d_win_ref,
):
    image = pl.program_id(0)
    width = d_context_ref.shape[1]
    groups = width // (PACK * HD)
    start = pl.multiple_of(image * STEP, ALIGN)

    @pl.when(image == 0)
    def _():
        d_mixed_ref[...] = jnp.zeros_like(d_mixed_ref)
        d_bias_ref[...] = jnp.zeros_like(d_bias_ref)
        d_qv_ref[...] = jnp.zeros_like(d_qv_ref)

    d_ctx_ref[...] = matmul(perm_ref[0], d_context_ref[pl.ds(start, SPAN), :]).astype(jnp.bfloat16)
    for g in range(groups):
        low = g * PACK * HD
        cols = slice(low, low + PACK * HD)
        d_bias = jnp.zeros((SLOT, PACK * SLOT), jnp.float32)
        d_query_sum = jnp.zeros((1, PACK * HD), jnp.float32)
        d_value_sum = jnp.zeros((1, PACK * HD), jnp.float32)
        for w in range(WIN_COUNT):
            rows = slice(w * SLOT, (w + 1) * SLOT)
            query = windows_ref[0, rows, low : low + PACK * HD]
            keys = windows_ref[0, rows, width + low : width + low + PACK * HD]
            values = windows_ref[0, rows, 2 * width + low : 2 * width + low + PACK * HD]
            probs = probs_ref[0, w * groups + g]
            d_wide = spread(d_ctx_ref[rows, cols], owner_ref[...])
            d_probs = matmul_nt(values, d_wide)
            d_values = matmul(probs.astype(jnp.bfloat16), d_wide)
            d_scores = probs * (d_probs - jnp.sum(probs * d_probs, 0, keepdims=True))
            d_bias = d_bias + d_scores
            d_low = d_scores.astype(jnp.bfloat16)
            d_keys = matmul(d_low, spread(query, owner_ref[...])) * HD ** (-0.5)
            d_query = gather_heads(matmul_tn(d_low, keys)) * HD ** (-0.5)
            d_win_ref[rows, low : low + PACK * HD] = d_query.astype(jnp.bfloat16)
            d_win_ref[rows, width + low : width + low + PACK * HD] = d_keys.astype(jnp.bfloat16)
            d_win_ref[rows, 2 * width + low : 2 * width + low + PACK * HD] = d_values.astype(jnp.bfloat16)
            d_query_sum = d_query_sum + jnp.sum(d_query, 0, keepdims=True)
            d_value_sum = d_value_sum + jnp.sum(d_values, 0, keepdims=True)
        d_bias_ref[g] += d_bias
        d_qv_ref[0:1, cols] += d_query_sum
        d_qv_ref[1:2, cols] += d_value_sum
    d_mixed_ref[pl.ds(start, SPAN), :] += matmul(perm_t_ref[0], d_win_ref[...]).astype(jnp.bfloat16)


def whole(shape):
    return pl.BlockSpec(shape, lambda n: (0,) * len(shape))


def per_image(shape):
    return pl.BlockSpec((1,) + shape, lambda n: (n,) + (0,) * len(shape))


def attend_forward(qkv, tables, bias, later):
    perm, perm_t, owner, _ = tables
    tok, wide = qkv.shape
    width = wide // 3
    count, spots = perm.shape[:2]
    tiles = WIN_COUNT * width // (PACK * HD)
    sizes = mesh_sizes()
    copies = len(later) * (sizes[0] - 1) + sizes[1] - 1
    proj_rows, fc1_rows, fc2_local = later
    shapes = [(rows.shape[0] * sizes[0], columns) for rows, columns in zip(later, (proj_rows.shape[1], fc1_rows.shape[1], fc2_local.shape[1] * sizes[1]))]
    return pl.pallas_call(
        functools.partial(forward_stage, sizes),
        grid=(count,),
        in_specs=[whole(qkv.shape), per_image((spots, SPAN)), per_image((SPAN, spots)), whole(bias.shape), whole(owner.shape)]
        + [whole(rows.shape) for rows in later],
        out_specs=[whole((tok, width)), per_image((spots, wide)), per_image((tiles, SLOT, PACK * SLOT))] + [hbm_spec()] * len(later),
        out_shape=[
            jax.ShapeDtypeStruct((tok, width), jnp.bfloat16),
            pltpu.HBM((count, spots, wide), jnp.bfloat16),
            pltpu.HBM((count, tiles, SLOT, PACK * SLOT), jnp.float32),
        ]
        + [jax.ShapeDtypeStruct(shape, jnp.bfloat16) for shape in shapes],
        scratch_shapes=[
            pltpu.VMEM((spots, width), jnp.bfloat16),
            pltpu.VMEM((sizes[1],) + later[2].shape, jnp.bfloat16),
            pltpu.VMEM((later[2].shape[0], later[2].shape[1] * sizes[1]), jnp.bfloat16),
            pltpu.SemaphoreType.DMA((copies,)),
            pltpu.SemaphoreType.DMA((copies,)),
            pltpu.SemaphoreType.DMA((len(later),)),
            pltpu.SemaphoreType.DMA((1,)),
        ],
        compiler_params=pltpu.CompilerParams(collective_id=2, has_side_effects=True, vmem_limit_bytes=FWD_GRANT),
        cost_estimate=pl.CostEstimate(flops=6_000_000_000, bytes_accessed=24_000_000, transcendentals=tok * width * 2),
        name="attend_forward",
    )(qkv, perm, perm_t, bias, owner, *later)


def attend_backward(d_context, windows, probs, tables, sums):
    perm, perm_t, owner, onehot = tables
    tok, width = d_context.shape
    count, spots, wide = windows.shape
    groups = width // (PACK * HD)
    tiles = probs.shape[1]
    sizes = mesh_sizes()
    blocks = [(full.shape[0] // sizes[0], full.shape[1]) for full in sums]
    halves = [
        pltpu.VMEM((sizes[0] >> (bit + 1),) + block, jnp.bfloat16) for block in blocks for bit in range(bits_of(sizes[0]))
    ]
    copies = len(sums) * (sizes[0] - 1)
    d_mixed, d_bias, d_qv, *sums = pl.pallas_call(
        functools.partial(backward_stage, sizes),
        grid=(count,),
        in_specs=[
            whole(d_context.shape), per_image((spots, wide)), per_image((tiles, SLOT, PACK * SLOT)),
            per_image((spots, SPAN)), per_image((SPAN, spots)), whole(owner.shape),
        ]
        + [whole(full.shape) for full in sums],
        out_specs=[whole((tok, wide)), whole((groups, SLOT, PACK * SLOT)), whole((2, width))] + [whole(block) for block in blocks],
        out_shape=[
            jax.ShapeDtypeStruct((tok, wide), jnp.bfloat16),
            jax.ShapeDtypeStruct((groups, SLOT, PACK * SLOT), jnp.float32),
            jax.ShapeDtypeStruct((2, width), jnp.float32),
        ]
        + [jax.ShapeDtypeStruct(block, jnp.bfloat16) for block in blocks],
        scratch_shapes=[pltpu.VMEM((spots, width), jnp.bfloat16), pltpu.VMEM((spots, wide), jnp.bfloat16)]
        + halves
        + [pltpu.SemaphoreType.DMA((copies,)), pltpu.SemaphoreType.DMA((copies,))],
        compiler_params=pltpu.CompilerParams(collective_id=3, has_side_effects=True, vmem_limit_bytes=BWD_GRANT),
        cost_estimate=pl.CostEstimate(flops=9_000_000_000, bytes_accessed=32_000_000, transcendentals=0),
        name="attend_backward",
    )(d_context, windows, probs, perm, perm_t, owner, *sums)
    d_bias = d_bias.reshape(groups, SLOT, PACK, SLOT).transpose(0, 2, 1, 3).reshape(groups * PACK, SLOT * SLOT)
    d_table = lax.dot_general(
        onehot.astype(jnp.float32), d_bias, (((1,), (1,)), ((), ())), precision=lax.Precision.HIGHEST
    )
    return d_mixed, d_qv, d_table, sums


def gelu_parts(pre_act):
    cdf_part = 0.5 * (1.0 + jax.scipy.special.erf(pre_act * inv_root_two))
    return (
        pre_act * cdf_part,
        cdf_part + pre_act * jnp.exp(-0.5 * pre_act * pre_act) * inv_root_two_pi,
    )


def layer_norm(rows, gain, shift):
    row_mean = jnp.mean(rows, -1, keepdims=True)
    row_var = jnp.mean(rows * rows, -1, keepdims=True) - row_mean * row_mean
    inv_std = lax.rsqrt(row_var + eps_norm)
    normed = (rows - row_mean) * inv_std
    return (normed, inv_std, normed * gain + shift)


def norm_back(d_out, normed, inv_std, gain):
    d_normed = d_out * gain
    return inv_std * (
        d_normed
        - jnp.mean(d_normed, -1, keepdims=True)
        - normed * jnp.mean(d_normed * normed, -1, keepdims=True)
    )


ROW_PAD = 16
FWD_GRANT = 16 << 20
BWD_GRANT = 24 << 20


def bit_of(index, bit):
    return (index // (1 << bit)) % 2


def bits_of(size):
    return size.bit_length() - 1


def greet(gx_size, gy_size):
    mine, row = lax.axis_index("gx"), lax.axis_index("gy")
    barrier = pltpu.get_barrier_semaphore()
    for bit in range(bits_of(gx_size)):
        there = mine + (1 << bit) * (1 - 2 * bit_of(mine, bit))
        pl.semaphore_signal(barrier, inc=1, device_id={"gx": there}, device_id_type=pl.DeviceIdType.MESH)
    for away in range(1, gy_size):
        there = (row + away) % gy_size
        pl.semaphore_signal(barrier, inc=1, device_id={"gy": there}, device_id_type=pl.DeviceIdType.MESH)
    pl.semaphore_wait(barrier, bits_of(gx_size) + gy_size - 1)


class Sender:
    def __init__(self, send, recv):
        self.send, self.recv, self.used = send, recv, 0

    def plan(self, src, dst, name, there):
        copy = pltpu.make_async_remote_copy(
            src_ref=src,
            dst_ref=dst,
            send_sem=self.send.at[self.used],
            recv_sem=self.recv.at[self.used],
            device_id={name: there},
            device_id_type=pl.DeviceIdType.MESH,
        )
        self.used += 1
        return copy


def phase(waits=(), act=None, starts=()):
    def run():
        for copy in waits:
            copy.wait()
        if act is not None:
            act()
        for copy in starts:
            copy.start()

    return run


def split_steps(index, size):
    top = bits_of(size) - 1
    core = index % 2
    high, low = bit_of(index, top), bit_of(index, top - 1)
    big, small = 1 << top, 1 << (top - 1)
    first_step = (1 - core) * big * (1 - 2 * high) + core * small * (1 - 2 * low)
    second_step = (1 - core) * small * (1 - 2 * low) + core * big * (1 - 2 * high)
    return core, high, low, first_step, second_step


def gather_column(sender, local, slots, sem, sizes, act=None):
    row = lax.axis_index("gy")
    own = [pltpu.make_async_copy(ref, slot.at[row], sem.at[n]) for n, (ref, slot) in enumerate(zip(local, slots))]
    copies = [
        sender.plan(ref, slot.at[row], "gy", (row + away) % sizes[1])
        for ref, slot in zip(local, slots)
        for away in range(1, sizes[1])
    ]
    return [phase((), None, own + copies), phase(own + copies, act)]


def join_rows(slots, rows_ref, groups):
    gy_size, _, wide = slots.shape
    width = wide // groups
    for i in range(gy_size):
        for k in range(groups):
            low = (k * gy_size + i) * width
            rows_ref[:, low : low + width] = slots[i, :, k * width : (k + 1) * width]


def gather_plane(sender, own, full, sem, sizes):
    gx_size = sizes[0]
    mine = lax.axis_index("gx")
    rows = own.shape[0]
    core, _, _, first_step, second_step = split_steps(mine, gx_size)
    steps = [first_step, second_step]
    for bit in range(1, bits_of(gx_size) - 2)[::-1]:
        steps.append((1 << bit) * (1 - 2 * bit_of(mine, bit)))
    over = 1 - 2 * core

    def view(at):
        return full.at[pl.ds(pl.multiple_of(at * rows, rows), rows), :]

    def push(at, first, there):
        return sender.plan(own if first else view(at), view(at), "gx", there)

    keep = pltpu.make_async_copy(own, view(mine), sem)
    held, fresh = [mine], [mine]
    waits, shared, phases = [], [keep], []
    for place, step in enumerate(steps):
        copies = [push(at, n == 0, mine + step) for n, at in enumerate(held)]
        across = [push(at, place == 0, mine + over) for at in fresh]
        phases.append(phase(waits, None, copies + across + ([keep] if place == 0 else [])))
        waits = copies
        shared += across
        fresh = [at + step for at in held]
        held = held + fresh
    across = [push(at, False, mine + over) for at in fresh]
    phases.append(phase(waits, None, across))
    phases.append(phase(shared + across))
    return phases


def add_into(target, left, right):
    target[...] = (left[...].astype(jnp.float32) + right[...].astype(jnp.float32)).astype(target.dtype)


def add_arrived(copies, came, kept, out=None):
    def run():
        for k, (copy, view) in enumerate(zip(copies, kept)):
            copy.wait()
            add_into(came.at[k] if out is None else out, came.at[k], view)

    return run


def share_plane(sender, full, halves, out, sizes):
    gx_size = sizes[0]
    mine = lax.axis_index("gx")
    rows = full.shape[0] // gx_size
    core, high, low, first_step, second_step = split_steps(mine, gx_size)

    def block(at):
        return full.at[pl.ds(pl.multiple_of(at * rows, rows), rows), :]

    held, act, phases = block, None, []
    count = gx_size
    for bit in range(bits_of(gx_size)):
        came = halves[bit]
        count //= 2
        own = bit_of(mine, bit)
        if count >= 4:
            step = (1 << bit) * (1 - 2 * own)
            away = [2 * k + 1 - own for k in range(count)]
            kept = [2 * k + own for k in range(count)]
        elif count == 2:
            step = second_step
            away = [(1 - core) * (2 * k + 1 - low) + core * (2 * (1 - high) + k) for k in range(count)]
            kept = [(1 - core) * (2 * k + low) + core * (2 * high + k) for k in range(count)]
        else:
            step = first_step
            last = (1 - core) * high + core * low
            away, kept = [1 - last], [last]
        copies = [sender.plan(held(at), came.at[k], "gx", mine + step) for k, at in enumerate(away)]
        phases.append(phase((), act, copies))
        act = add_arrived(copies, came, [held(at) for at in kept], out if count == 1 else None)
        held = (lambda ref: lambda at: ref.at[at])(came)
    phases.append(phase((), act))
    return phases


def share_column(sender, total, slots, came, out, groups, sizes):
    gy_size = sizes[1]
    row = lax.axis_index("gy")
    width = slots.shape[2] // groups

    def split():
        for i in range(gy_size):
            for k in range(groups):
                low = (k * gy_size + i) * width
                slots[i, :, k * width : (k + 1) * width] = total[:, low : low + width]

    targets = [(row + away) % gy_size for away in range(1, gy_size)]
    copies = [sender.plan(slots.at[there], came.at[n], "gy", there) for n, there in enumerate(targets)]

    def finish():
        total = slots[row].astype(jnp.float32)
        for n, copy in enumerate(copies):
            copy.wait()
            total = total + came[n].astype(jnp.float32)
        out[...] = total

    return [phase((), split, copies), phase((), finish)]


def sum_small(sender, value, came, totals, column, out, sizes):
    held, act, phases = value, None, []
    mine, row = lax.axis_index("gx"), lax.axis_index("gy")
    for bit in range(bits_of(sizes[0])):
        there = mine + (1 << bit) * (1 - 2 * bit_of(mine, bit))
        copy = sender.plan(held, came.at[bit], "gx", there)
        phases.append(phase((), act, [copy]))
        act = add_small(copy, held, came, bit, totals.at[bit])
        held = totals.at[bit]
    copies = [sender.plan(held, column.at[row], "gy", (row + away) % sizes[1]) for away in range(1, sizes[1])]
    phases.append(phase((), act, copies))

    def finish():
        column[row] = held[...]
        for copy in copies:
            copy.wait()
        total = column[0]
        for i in range(1, sizes[1]):
            total = total + column[i]
        out[...] = total

    phases.append(phase((), finish))
    return phases


def add_small(copy, held, came, stage, target):
    def run():
        copy.wait()
        target[...] = held[...] + came[stage]

    return run


def fill_bias(small_all, rel_ref, mask_ref, bias_ref, spread_ref, heads_local):
    gy_size, pad_rows, lanes = small_all.shape
    depth = -(-RELS // 16) * 16
    onehot = (lax.broadcasted_iota(jnp.int32, (depth, SLOT * SLOT), 0) == rel_ref[...]).astype(jnp.bfloat16)
    table = small_all[...].reshape(gy_size * pad_rows, lanes)[:, :depth]
    wide = matmul(table, onehot)
    total = gy_size * pad_rows
    for j in range(SLOT):
        spread_ref[j * total : (j + 1) * total, :] = wide[:, j * SLOT : (j + 1) * SLOT]
    for h in range(gy_size * heads_local):
        line = h // heads_local * pad_rows + 2 + h % heads_local
        one = spread_ref[pl.ds(line, SLOT, stride=total), :]
        low = h % PACK * SLOT
        for w in range(WIN_COUNT):
            bias_ref[w, h // PACK, :, low : low + SLOT] = one + mask_ref[w]


def gather_kernel(sizes, heads_local, qkv_ref, small_ref, proj_ref, fc1_ref, rel_ref, mask_ref,
                  qkv_full, small_all, bias_ref, proj_rows, fc1_rows,
                  qkv_slots, proj_slots, fc1_slots, qkv_rows, spread_ref, send, recv, own_sem, keep_sem):
    greet(*sizes)
    sender = Sender(send, recv)

    def join_later():
        join_rows(proj_slots, proj_rows, 1)
        join_rows(fc1_slots, fc1_rows, 1)

    first = gather_column(sender, [small_ref, qkv_ref], [small_all, qkv_slots], own_sem.at[0], sizes, lambda: join_rows(qkv_slots, qkv_rows, 3))
    second = gather_column(sender, [proj_ref, fc1_ref], [proj_slots, fc1_slots], own_sem.at[1], sizes, join_later)
    plane = gather_plane(sender, qkv_rows, qkv_full, keep_sem.at[0], sizes)
    first[0]()
    second[0]()
    first[1]()
    plane[0]()
    fill_bias(small_all, rel_ref, mask_ref, bias_ref, spread_ref, heads_local)
    for run in plane[1:]:
        run()
    second[1]()


def vmem_spec():
    return pl.BlockSpec(memory_space=pltpu.VMEM)


def hbm_spec():
    return pl.BlockSpec(memory_space=pl.ANY)


def mesh_sizes():
    return lax.axis_size("gx"), lax.axis_size("gy")


def gather_weights(qkv, small, proj_t, fc1, heads_local):
    sizes = mesh_sizes()
    gx_size, gy_size = sizes
    rows = qkv.shape[0]
    _, rel, mask = static_tables(1)
    later = [jax.ShapeDtypeStruct((rows, v.shape[1] * gy_size), v.dtype) for v in (proj_t, fc1)]
    wide = qkv.shape[1] * gy_size
    count = 4 * (gy_size - 1) + gx_size - 1
    bias = (WIN_COUNT, gy_size * heads_local // PACK, SLOT, PACK * SLOT)
    return pl.pallas_call(
        functools.partial(gather_kernel, sizes, heads_local),
        in_specs=[hbm_spec()] * 4 + [vmem_spec()] * 2,
        out_specs=[hbm_spec()] + [vmem_spec()] * 4,
        out_shape=[
            jax.ShapeDtypeStruct((rows * gx_size, wide), qkv.dtype),
            jax.ShapeDtypeStruct((gy_size,) + small.shape, small.dtype),
            jax.ShapeDtypeStruct(bias, jnp.float32),
        ]
        + later,
        scratch_shapes=[pltpu.VMEM((gy_size,) + v.shape, v.dtype) for v in (qkv, proj_t, fc1)]
        + [
            pltpu.VMEM((rows, wide), qkv.dtype),
            pltpu.VMEM((SLOT * gy_size * small.shape[0], SLOT), jnp.float32),
            pltpu.SemaphoreType.DMA((count,)), pltpu.SemaphoreType.DMA((count,)), pltpu.SemaphoreType.DMA((2, 2)),
            pltpu.SemaphoreType.DMA((1,)),
        ],
        compiler_params=pltpu.CompilerParams(collective_id=0, has_side_effects=True, vmem_limit_bytes=14 << 20),
        name="gather_weights",
    )(qkv, small, proj_t, fc1, jnp.asarray(rel.reshape(1, -1)), jnp.asarray(mask))


def share_kernel(sizes, groups, whole_count, *refs):
    gx_bits = bits_of(sizes[0])
    arrays = len(groups)
    refs = list(refs)

    def take(count):
        out = refs[:count]
        del refs[:count]
        return out

    inputs, (small,) = take(arrays), take(1)
    act, fc2_full, resid, shift = take(4)
    outs, (small_out, output) = take(arrays), take(2)
    planes = [take(gx_bits) for _ in range(whole_count)]
    totals, slots, columns = take(whole_count), take(arrays), take(arrays)
    small_came, small_totals, small_column, send, recv = take(5)
    greet(*sizes)
    sender = Sender(send, recv)
    streams = []
    for n in range(arrays):
        phases = share_plane(sender, inputs[n], planes[n], totals[n], sizes) if n < whole_count else []
        total = totals[n] if n < whole_count else inputs[n]
        column = share_column(sender, total, slots[n], columns[n], outs[n], groups[n], sizes)
        if phases:
            last, after = phases.pop(), column.pop(0)
            phases.append(both(last, after))
        streams.append(phases + column)
    streams.append(sum_small(sender, small, small_came, small_totals, small_column, small_out, sizes))
    width = output.shape[1]
    chunk = min(2 * 128, width)
    rest = list(range(0, width, chunk))
    place = 0
    while any(streams):
        for queue in streams:
            if queue:
                queue.pop(0)()
        place += 1
        if place >= 2 and rest:
            low = rest.pop(0)
            cols = slice(low, low + chunk)
            output[:, cols] = (resid[:, cols] + matmul_nt(act[...], fc2_full[cols, :]) + shift[:, cols]).astype(output.dtype)
    for low in rest:
        cols = slice(low, low + chunk)
        output[:, cols] = (resid[:, cols] + matmul_nt(act[...], fc2_full[cols, :]) + shift[:, cols]).astype(output.dtype)


def both(one, other):
    def run():
        one()
        other()

    return run


def share_sums(fulls, rows_sums, groups, small, product):
    sizes = mesh_sizes()
    gx_size, gy_size = sizes
    gx_bits = bits_of(gx_size)
    rows = fulls[0].shape[0] // gx_size
    arrays = tuple(fulls) + tuple(rows_sums)
    planes, slots, columns = [], [], []
    for full in fulls:
        planes += [pltpu.VMEM((gx_size >> (bit + 1), rows, full.shape[1]), full.dtype) for bit in range(gx_bits)]
    for value in arrays:
        wide = value.shape[1] // gy_size
        slots.append(pltpu.VMEM((gy_size, rows, wide), value.dtype))
        columns.append(pltpu.VMEM((gy_size - 1, rows, wide), value.dtype))
    count = len(fulls) * (gx_size - 1) + len(arrays) * (gy_size - 1) + gx_bits + gy_size - 1
    return pl.pallas_call(
        functools.partial(share_kernel, sizes, groups, len(fulls)),
        in_specs=[vmem_spec()] * (len(arrays) + 5),
        out_specs=[vmem_spec()] * (len(arrays) + 2),
        out_shape=[jax.ShapeDtypeStruct((rows, value.shape[1] // gy_size), jnp.float32) for value in arrays]
        + [jax.ShapeDtypeStruct(small.shape, small.dtype), jax.ShapeDtypeStruct(product[2].shape, jnp.bfloat16)],
        scratch_shapes=planes + [pltpu.VMEM((rows, full.shape[1]), full.dtype) for full in fulls] + slots + columns + [
            pltpu.VMEM((gx_bits,) + small.shape, small.dtype),
            pltpu.VMEM((gx_bits,) + small.shape, small.dtype),
            pltpu.VMEM((gy_size,) + small.shape, small.dtype),
            pltpu.SemaphoreType.DMA((count,)),
            pltpu.SemaphoreType.DMA((count,)),
        ],
        compiler_params=pltpu.CompilerParams(collective_id=1, has_side_effects=True, vmem_limit_bytes=18 << 20),
        name="share_sums",
    )(*arrays, small, *product)


def forward_stage(
    sizes, qkv_ref, perm_ref, perm_t_ref, bias_ref, owner_ref, proj_rows, fc1_rows, fc2_local,
    context_ref, windows_ref, probs_ref, proj_full, fc1_full, fc2_full,
    ctx_ref, fc2_slots, fc2_rows, send, recv, keep_sem, own_sem,
):
    image, last = pl.program_id(0), pl.num_programs(0) - 1

    @pl.when(image == 0)
    def _():
        greet(*sizes)

    sender = Sender(send, recv)
    own = (proj_rows, fc1_rows, fc2_rows)
    fulls = (proj_full, fc1_full, fc2_full)
    streams = [gather_plane(sender, own[n], fulls[n], keep_sem.at[n], sizes) for n in range(3)]
    column = gather_column(sender, [fc2_local], [fc2_slots], own_sem, sizes, lambda: join_rows(fc2_slots, fc2_rows, 1))

    @pl.when(image == 0)
    def _():
        column[0]()
        streams[0][0]()
        streams[1][0]()

    @pl.when(image == jnp.minimum(1, last))
    def _():
        streams[0][1]()

    @pl.when(image == jnp.minimum(2, last))
    def _():
        streams[1][1]()
        column[1]()
        streams[2][0]()

    forward_kernel(
        qkv_ref, perm_ref, perm_t_ref, bias_ref, owner_ref, context_ref, windows_ref, probs_ref, ctx_ref
    )

    @pl.when(image == last)
    def _():
        streams[2][1]()
        for place in range(2, len(streams[0])):
            for phases in streams:
                phases[place]()


def backward_stage(
    sizes, d_context_ref, windows_ref, probs_ref, perm_ref, perm_t_ref, owner_ref, d_fc1_ref, d_fc2_ref,
    d_mixed_ref, d_bias_ref, d_qv_ref, fc1_sum, fc2_sum, d_ctx_ref, d_win_ref, *rest,
):
    image, last = pl.program_id(0), pl.num_programs(0) - 1
    gx_bits = bits_of(sizes[0])
    fc1_halves, fc2_halves, (send, recv) = rest[:gx_bits], rest[gx_bits : 2 * gx_bits], rest[2 * gx_bits :]

    @pl.when(image == 0)
    def _():
        greet(*sizes)

    sender = Sender(send, recv)
    streams = [
        share_plane(sender, d_fc1_ref, fc1_halves, fc1_sum, sizes),
        share_plane(sender, d_fc2_ref, fc2_halves, fc2_sum, sizes),
    ]

    @pl.when(image == 0)
    def _():
        for phases in streams:
            phases[0]()

    @pl.when(image == jnp.minimum(1, last))
    def _():
        for phases in streams:
            phases[1]()

    @pl.when(image == last)
    def _():
        streams[0][2]()

    backward_kernel(
        d_context_ref, windows_ref, probs_ref, perm_ref, perm_t_ref, owner_ref,
        d_mixed_ref, d_bias_ref, d_qv_ref, d_ctx_ref, d_win_ref,
    )

    @pl.when(image == last)
    def _():
        streams[1][2]()
        for place in range(3, len(streams[0])):
            for phases in streams:
                phases[place]()


def pack_rows(values):
    rows = []
    for value in values:
        flat = value.reshape(-1)
        rows.append(jnp.pad(flat, (0, -flat.shape[0] % 1024)).reshape(-1, 128))
    return jnp.concatenate(rows, 0)


def unpack_rows(packed, shapes):
    at, out = 0, []
    for shape in shapes:
        size = int(np.prod(shape))
        count = (size + 1023) // 1024 * 8
        out.append(packed[at : at + count].reshape(-1)[:size].reshape(shape))
        at += count
    return out


def own_columns(summed, axis):
    size = summed.shape[axis] // lax.axis_size("gy")
    return lax.dynamic_slice_in_dim(summed, lax.axis_index("gy") * size, size, axis)


def local_live(tok_local, live_images):
    position = lax.axis_index("gy")
    per_device = tok_local // (GRID * GRID)
    slot_index = position * per_device + jnp.arange(tok_local, dtype=jnp.int32) // (GRID * GRID)
    return slot_index < live_images[0]


def blocked_layer(block_input, cotangent, live_images, params):
    (
        ln1_gain,
        ln1_bias,
        qkv_weight,
        qv_bias,
        rel_table,
        proj_weight,
        proj_bias,
        ln2_gain,
        ln2_bias,
        fc1_weight,
        fc1_bias,
        fc2_weight,
        fc2_bias,
    ) = params
    tok_local, width = block_input.shape
    block_rows = qkv_weight.shape[0]
    part, hidden_local = qkv_weight.shape[2], fc1_weight.shape[1]
    heads_local = rel_table.shape[1]

    def lane_row(value):
        value = value.reshape(value.shape[0], -1)
        return jnp.pad(value, ((0, 0), (0, hidden_local - value.shape[1])))

    small = jnp.concatenate([fc1_bias[None], lane_row(qv_bias.reshape(1, -1)), lane_row(rel_table.T)], 0)
    small = jnp.pad(small, ((0, ROW_PAD - small.shape[0]), (0, 0)))
    qkv_flat, small, bias, *later = gather_weights(
        qkv_weight.reshape(block_rows, -1), small, proj_weight.T, fc1_weight, heads_local
    )
    later.append(fc2_weight.T)
    fc1_bias = small[:, 0].reshape(-1)
    qv_bias = small[:, 1, : 2 * part].reshape(-1, 2, part).transpose(1, 0, 2).reshape(2, -1)
    gain_one = ln1_gain.astype(jnp.float32)
    gain_two = ln2_gain.astype(jnp.float32)
    resid = block_input.astype(jnp.float32)
    normed_one, scale_one, pre_one = layer_norm(resid, gain_one, ln1_bias.astype(jnp.float32))
    hidden_one = (pre_one.astype(jnp.bfloat16))
    bias_row = jnp.stack([qv_bias[0], jnp.zeros_like(qv_bias[0]), qv_bias[1]]).reshape(1, 3 * width)
    mixed = (matmul(hidden_one, qkv_flat) + bias_row.astype(jnp.float32)).astype(jnp.bfloat16)
    tables = attention_tables(tok_local // IMAGE)
    context, windows, probs, proj_cols, fc1_rows, fc2_cols = attend_forward(mixed, tables, bias, later)
    resid_one = resid + (matmul_nt(context, proj_cols)) + proj_bias.astype(jnp.float32)
    normed_two, scale_two, pre_two = layer_norm(resid_one, gain_two, ln2_bias.astype(jnp.float32))
    hidden_two = (pre_two.astype(jnp.bfloat16))
    pre_act = matmul(hidden_two, fc1_rows) + fc1_bias.astype(jnp.float32)
    act_full, slope = gelu_parts(pre_act)
    act_low = act_full.astype(jnp.bfloat16)
    live_rows = local_live(tok_local, live_images)
    grad_out = jnp.where(live_rows[:, None], cotangent, jnp.zeros_like(cotangent))
    grad_float = grad_out.astype(jnp.float32)
    grad_full = (grad_out)
    d_fc2_bias = jnp.sum(grad_float, 0)
    d_fc2_weight = matmul_tn(grad_full, act_low).astype(jnp.bfloat16)
    d_pre = matmul(grad_full, fc2_cols) * slope
    d_fc1_bias = jnp.sum(d_pre, 0)
    d_pre_low = d_pre.astype(jnp.bfloat16)
    d_fc1_weight = matmul_tn(hidden_two, d_pre_low).astype(jnp.bfloat16)
    d_hidden_two = (matmul_nt(d_pre_low, fc1_rows))
    d_ln2_gain = jnp.sum(d_hidden_two * normed_two, 0)
    d_ln2_bias = jnp.sum(d_hidden_two, 0)
    d_resid_one = grad_float + norm_back(d_hidden_two, normed_two, scale_two, gain_two)
    d_proj_bias = jnp.sum(d_resid_one, 0)
    d_resid_full = (d_resid_one.astype(jnp.bfloat16))
    d_proj_weight = matmul_tn(d_resid_full, context).astype(jnp.bfloat16)
    d_context = matmul(d_resid_full, proj_cols).astype(jnp.bfloat16)
    d_mixed, d_qv_bias, d_table, sums = attend_backward(d_context, windows, probs, tables, (d_fc1_weight, d_fc2_weight))
    d_qkv_weight = matmul_tn(hidden_one, d_mixed).astype(jnp.bfloat16)
    d_hidden_one = (matmul_nt(d_mixed, qkv_flat))
    d_ln1_gain = jnp.sum(d_hidden_one * normed_one, 0)
    d_ln1_bias = jnp.sum(d_hidden_one, 0)
    d_input = (d_resid_one + norm_back(d_hidden_one, normed_one, scale_one, gain_one)).astype(
        jnp.bfloat16
    )
    own = (d_ln1_gain, d_ln1_bias, d_proj_bias, d_ln2_gain, d_ln2_bias, d_fc2_bias, d_qv_bias, d_table, d_fc1_bias)
    product = (act_low, fc2_cols, resid_one, fc2_bias.astype(jnp.float32)[None])
    d_qkv_weight, d_proj_weight, d_fc1_weight, d_fc2_weight, sums, output = share_sums(
        (d_qkv_weight, d_proj_weight), sums, (3, 1, 1, 1), pack_rows(own), product
    )
    d_fc2_weight = d_fc2_weight.T
    d_proj_weight = d_proj_weight.T
    d_qkv_weight = d_qkv_weight.reshape(block_rows, 3, part)
    sums = unpack_rows(sums, [value.shape for value in own])
    norm_sums = sums[:6]
    head_sums = (own_columns(sums[6], 1), own_columns(sums[7], 1), own_columns(sums[8], 0))
    return (
        output,
        d_input,
        norm_sums[0],
        norm_sums[1],
        d_qkv_weight,
        head_sums[0],
        head_sums[1],
        d_proj_weight,
        norm_sums[2],
        norm_sums[3],
        norm_sums[4],
        d_fc1_weight,
        head_sums[2],
        d_fc2_weight,
        norm_sums[5],
    )


def shards(
    block_input,
    cotangent,
    live_images,
    ln1_gain,
    ln1_bias,
    qkv_weight,
    qv_bias,
    rel_table,
    proj_weight,
    proj_bias,
    ln2_gain,
    ln2_bias,
    fc1_weight,
    fc1_bias,
    fc2_weight,
    fc2_bias,
):
    params = (
        ln1_gain,
        ln1_bias,
        qkv_weight,
        qv_bias,
        rel_table,
        proj_weight,
        proj_bias,
        ln2_gain,
        ln2_bias,
        fc1_weight,
        fc1_bias,
        fc2_weight,
        fc2_bias,
    )
    return blocked_layer(block_input, cotangent, live_images, params)


def solution(mesh):
    return jax.shard_map(
        shards,
        mesh=mesh,
        in_specs=(
            P(("gx", "gy"), None),
            P(("gx", "gy"), None),
            P("gx"),
            P(),
            P(),
            P("gx", None, "gy"),
            P(None, "gy"),
            P(None, "gy"),
            P("gy", "gx"),
            P(),
            P(),
            P(),
            P("gx", "gy"),
            P("gy"),
            P("gy", "gx"),
            P(),
        ),
        out_specs=(
            P(("gx", "gy"), None),
            P(("gx", "gy"), None),
            P(),
            P(),
            P("gx", None, "gy"),
            P(None, "gy"),
            P(None, "gy"),
            P("gy", "gx"),
            P(),
            P(),
            P(),
            P("gx", "gy"),
            P("gy"),
            P("gy", "gx"),
            P(),
        ),
        check_vma=False,
    )
```

```python
import functools
import jax
import jax.numpy as jnp
from jax import lax
import numpy as np
from jax.experimental import pallas as pl
from jax.experimental.pallas import tpu as pltpu
from jax.sharding import PartitionSpec as P

HD = 32
GRID = 14
WIN = 7
SHIFT = 3
RELS = 169


eps_norm = 1e-05
mask_value = -100.0
inv_root_two = 0.7071067811865476
inv_root_two_pi = 0.3989422804014327


def matmul(left, right):
    return jnp.dot(left, right, preferred_element_type=jnp.float32)


def matmul_tn(left, right):
    return lax.dot_general(
        left, right, (((0,), (0,)), ((), ())), preferred_element_type=jnp.float32
    )


def matmul_nt(left, right):
    return lax.dot_general(
        left, right, (((1,), (1,)), ((), ())), preferred_element_type=jnp.float32
    )


SLOT = 64
PACK = 8
WIN_COUNT = (GRID // WIN) ** 2
IMAGE = GRID * GRID
ALIGN = 16
STEP = IMAGE // ALIGN * ALIGN
SPAN = STEP + ALIGN
far_below = -1e30


def static_tables(image_count):
    rows = np.arange(WIN_COUNT * SLOT)
    win, place = rows // SLOT, rows % SLOT
    row = (win // (GRID // WIN) * WIN + place // WIN + SHIFT) % GRID
    col = (win % (GRID // WIN) * WIN + place % WIN + SHIFT) % GRID
    token = np.where(place < WIN * WIN, row * GRID + col, -1)
    offset = np.arange(image_count) * (IMAGE - STEP)
    column = np.where(token[None] >= 0, token[None] + offset[:, None], -1)
    places = np.arange(SLOT)
    live = places < WIN * WIN
    pr, pc = places // WIN, places % WIN
    rel = (pr[None, :] - pr[:, None] + WIN - 1) * (2 * WIN - 1) + pc[None, :] - pc[:, None] + WIN - 1
    rel = np.where(live[:, None] & live[None, :], rel, -1)
    cells = np.arange(GRID)
    region = np.where(cells < GRID - WIN, 0, np.where(cells < GRID - SHIFT, 1, 2))
    shifted_row = (win // (GRID // WIN) * WIN + np.minimum(place // WIN, WIN - 1)).reshape(WIN_COUNT, SLOT)
    shifted_col = (win % (GRID // WIN) * WIN + place % WIN).reshape(WIN_COUNT, SLOT)
    ids = region[shifted_row] * 3 + region[shifted_col]
    mask = np.where(ids[:, :, None] == ids[:, None, :], 0.0, mask_value)
    mask = np.where(live[None, None, :] & live[None, :, None], mask, 0.0)
    mask = np.where(live[None, :, None], mask, far_below)
    return column.astype(np.int32), rel.astype(np.int32), mask.astype(np.float32)


def attention_tables(image_count):
    column, _, _ = static_tables(image_count)
    spots = np.arange(SPAN, dtype=np.int32)
    perm = jnp.asarray((column[:, :, None] == spots).astype(np.float32)).astype(jnp.bfloat16)
    perm_t = jnp.asarray((column[:, None, :] == spots[:, None]).astype(np.float32)).astype(jnp.bfloat16)
    owner = np.arange(PACK * SLOT)[:, None] // SLOT == np.arange(PACK * HD)[None, :] // HD
    owner = jnp.asarray(owner.astype(np.float32)).astype(jnp.bfloat16)
    return perm, perm_t, owner


def spread(rows, owner):
    return jnp.concatenate([rows] * PACK, axis=0) * owner


def gather_heads(full):
    lanes = lax.broadcasted_iota(jnp.int32, (SLOT, PACK * HD), 1) // HD
    total = full[:SLOT]
    for h in range(1, PACK):
        total = jnp.where(lanes == h, full[h * SLOT : (h + 1) * SLOT], total)
    return total


def forward_kernel(qkv_ref, perm_ref, perm_t_ref, bias_ref, owner_ref, context_ref, windows_ref, probs_ref, ctx_ref):
    image = pl.program_id(0)
    width = context_ref.shape[1]
    groups = width // (PACK * HD)
    start = pl.multiple_of(image * STEP, ALIGN)
    windows_ref[0] = matmul(perm_ref[0], qkv_ref[pl.ds(start, SPAN), :]).astype(jnp.bfloat16)
    for w in range(WIN_COUNT):
        rows = slice(w * SLOT, (w + 1) * SLOT)
        for g in range(groups):
            low = g * PACK * HD
            query = windows_ref[0, rows, low : low + PACK * HD]
            keys = windows_ref[0, rows, width + low : width + low + PACK * HD]
            values = windows_ref[0, rows, 2 * width + low : 2 * width + low + PACK * HD]
            scores = matmul_nt(keys, spread(query, owner_ref[...])) * HD ** (-0.5) + bias_ref[w, g]
            raised = jnp.exp(scores - jnp.max(scores, 0, keepdims=True))
            probs = raised * (1.0 / jnp.sum(raised, 0, keepdims=True))
            probs_ref[0, w * groups + g] = probs
            full = matmul_tn(probs.astype(jnp.bfloat16), values)
            ctx_ref[rows, low : low + PACK * HD] = gather_heads(full).astype(jnp.bfloat16)

    @pl.when(image == 0)
    def _():
        context_ref[...] = jnp.zeros_like(context_ref)

    context_ref[pl.ds(start, SPAN), :] += matmul(perm_t_ref[0], ctx_ref[...]).astype(jnp.bfloat16)


def backward_kernel(
    d_context_ref, windows_ref, probs_ref, perm_ref, perm_t_ref, owner_ref,
    d_mixed_ref, d_bias_ref, d_qv_ref, d_ctx_ref, d_win_ref, between,
):
    image = pl.program_id(0)
    width = d_context_ref.shape[1]
    groups = width // (PACK * HD)
    start = pl.multiple_of(image * STEP, ALIGN)

    @pl.when(image == 0)
    def _():
        d_mixed_ref[...] = jnp.zeros_like(d_mixed_ref)
        d_bias_ref[...] = jnp.zeros_like(d_bias_ref)
        d_qv_ref[...] = jnp.zeros_like(d_qv_ref)

    d_ctx_ref[...] = matmul(perm_ref[0], d_context_ref[pl.ds(start, SPAN), :]).astype(jnp.bfloat16)
    for g in range(groups):
        between(2 * image + min(g, 1))
        low = g * PACK * HD
        cols = slice(low, low + PACK * HD)
        d_bias = jnp.zeros((SLOT, PACK * SLOT), jnp.float32)
        d_query_sum = jnp.zeros((1, PACK * HD), jnp.float32)
        d_value_sum = jnp.zeros((1, PACK * HD), jnp.float32)
        for w in range(WIN_COUNT):
            rows = slice(w * SLOT, (w + 1) * SLOT)
            query = windows_ref[0, rows, low : low + PACK * HD]
            keys = windows_ref[0, rows, width + low : width + low + PACK * HD]
            values = windows_ref[0, rows, 2 * width + low : 2 * width + low + PACK * HD]
            probs = probs_ref[0, w * groups + g]
            d_wide = spread(d_ctx_ref[rows, cols], owner_ref[...])
            d_probs = matmul_nt(values, d_wide)
            d_values = matmul(probs.astype(jnp.bfloat16), d_wide)
            d_scores = probs * (d_probs - jnp.sum(probs * d_probs, 0, keepdims=True))
            d_bias = d_bias + d_scores
            d_low = d_scores.astype(jnp.bfloat16)
            d_keys = matmul(d_low, spread(query, owner_ref[...])) * HD ** (-0.5)
            d_query = gather_heads(matmul_tn(d_low, keys)) * HD ** (-0.5)
            d_win_ref[rows, low : low + PACK * HD] = d_query.astype(jnp.bfloat16)
            d_win_ref[rows, width + low : width + low + PACK * HD] = d_keys.astype(jnp.bfloat16)
            d_win_ref[rows, 2 * width + low : 2 * width + low + PACK * HD] = d_values.astype(jnp.bfloat16)
            d_query_sum = d_query_sum + jnp.sum(d_query, 0, keepdims=True)
            d_value_sum = d_value_sum + jnp.sum(d_values, 0, keepdims=True)
        d_bias_ref[g] += d_bias
        d_qv_ref[0:1, cols] += d_query_sum
        d_qv_ref[1:2, cols] += d_value_sum
    d_mixed_ref[pl.ds(start, SPAN), :] += matmul(perm_t_ref[0], d_win_ref[...]).astype(jnp.bfloat16)


def whole(shape):
    return pl.BlockSpec(shape, lambda n: (0,) * len(shape))


def per_image(shape):
    return pl.BlockSpec((1,) + shape, lambda n: (n,) + (0,) * len(shape))


def attend_forward(qkv, tables, bias, later):
    perm, perm_t, owner = tables
    tok, wide = qkv.shape
    width = wide // 3
    count, spots = perm.shape[:2]
    tiles = WIN_COUNT * width // (PACK * HD)
    sizes = mesh_sizes()
    copies = len(later) * (sizes[0] - 1) + sizes[1] - 1
    proj_rows, fc1_rows, fc2_local = later
    shapes = [(rows.shape[0] * sizes[0], columns) for rows, columns in zip(later, (proj_rows.shape[1], fc1_rows.shape[1], fc2_local.shape[1] * sizes[1]))]
    return pl.pallas_call(
        functools.partial(forward_stage, sizes),
        grid=(count,),
        in_specs=[whole(qkv.shape), per_image((spots, SPAN)), per_image((SPAN, spots)), whole(bias.shape), whole(owner.shape)]
        + [whole(rows.shape) for rows in later],
        out_specs=[whole((tok, width)), per_image((spots, wide)), per_image((tiles, SLOT, PACK * SLOT))] + [hbm_spec()] * len(later),
        out_shape=[
            jax.ShapeDtypeStruct((tok, width), jnp.bfloat16),
            pltpu.HBM((count, spots, wide), jnp.bfloat16),
            pltpu.HBM((count, tiles, SLOT, PACK * SLOT), jnp.float32),
        ]
        + [jax.ShapeDtypeStruct(shape, jnp.bfloat16) for shape in shapes],
        scratch_shapes=[
            pltpu.VMEM((spots, width), jnp.bfloat16),
            pltpu.VMEM((sizes[1],) + later[2].shape, jnp.bfloat16),
            pltpu.VMEM((later[2].shape[0], later[2].shape[1] * sizes[1]), jnp.bfloat16),
            pltpu.SemaphoreType.DMA((copies,)),
            pltpu.SemaphoreType.DMA((copies,)),
            pltpu.SemaphoreType.DMA((len(later),)),
            pltpu.SemaphoreType.DMA((1,)),
        ],
        compiler_params=pltpu.CompilerParams(collective_id=2, has_side_effects=True, vmem_limit_bytes=FWD_GRANT),
        cost_estimate=pl.CostEstimate(flops=6_000_000_000, bytes_accessed=24_000_000, transcendentals=tok * width * 2),
        name="attend_forward",
    )(qkv, perm, perm_t, bias, owner, *later)


def attend_backward(d_context, windows, probs, tables, sums):
    perm, perm_t, owner = tables
    tok, width = d_context.shape
    count, spots, wide = windows.shape
    groups = width // (PACK * HD)
    tiles = probs.shape[1]
    sizes = mesh_sizes()
    blocks = [(full.shape[0] // sizes[0], full.shape[1]) for full in sums]
    halves = [
        pltpu.VMEM((sizes[0] >> (bit + 1),) + block, jnp.bfloat16) for block in blocks for bit in range(bits_of(sizes[0]))
    ]
    copies = len(sums) * (sizes[0] - 1)
    d_mixed, d_bias, d_qv, *sums = pl.pallas_call(
        functools.partial(backward_stage, sizes),
        grid=(count,),
        in_specs=[
            whole(d_context.shape), per_image((spots, wide)), per_image((tiles, SLOT, PACK * SLOT)),
            per_image((spots, SPAN)), per_image((SPAN, spots)), whole(owner.shape),
        ]
        + [whole(full.shape) for full in sums],
        out_specs=[whole((tok, wide)), whole((groups, SLOT, PACK * SLOT)), whole((2, width))] + [whole(block) for block in blocks],
        out_shape=[
            jax.ShapeDtypeStruct((tok, wide), jnp.bfloat16),
            jax.ShapeDtypeStruct((groups, SLOT, PACK * SLOT), jnp.float32),
            jax.ShapeDtypeStruct((2, width), jnp.float32),
        ]
        + [jax.ShapeDtypeStruct(block, jnp.bfloat16) for block in blocks],
        scratch_shapes=[pltpu.VMEM((spots, width), jnp.bfloat16), pltpu.VMEM((spots, wide), jnp.bfloat16)]
        + halves
        + [pltpu.SemaphoreType.DMA((copies,)), pltpu.SemaphoreType.DMA((copies,))],
        compiler_params=pltpu.CompilerParams(collective_id=3, has_side_effects=True, vmem_limit_bytes=BWD_GRANT),
        cost_estimate=pl.CostEstimate(flops=9_000_000_000, bytes_accessed=32_000_000, transcendentals=0),
        name="attend_backward",
    )(d_context, windows, probs, perm, perm_t, owner, *sums)
    return d_mixed, d_qv, d_bias, sums


def gelu_parts(pre_act):
    cdf_part = 0.5 * (1.0 + jax.scipy.special.erf(pre_act * inv_root_two))
    return (
        pre_act * cdf_part,
        cdf_part + pre_act * jnp.exp(-0.5 * pre_act * pre_act) * inv_root_two_pi,
    )


def layer_norm(rows, gain, shift):
    row_mean = jnp.mean(rows, -1, keepdims=True)
    row_var = jnp.mean(rows * rows, -1, keepdims=True) - row_mean * row_mean
    inv_std = lax.rsqrt(row_var + eps_norm)
    normed = (rows - row_mean) * inv_std
    return (normed, inv_std, normed * gain + shift)


def norm_back(d_out, normed, inv_std, gain):
    d_normed = d_out * gain
    return inv_std * (
        d_normed
        - jnp.mean(d_normed, -1, keepdims=True)
        - normed * jnp.mean(d_normed * normed, -1, keepdims=True)
    )


ROW_PAD = 16
FWD_GRANT = 16 << 20
BWD_GRANT = 24 << 20


def bit_of(index, bit):
    return (index // (1 << bit)) % 2


def bits_of(size):
    return size.bit_length() - 1


def greet(gx_size, gy_size):
    mine, row = lax.axis_index("gx"), lax.axis_index("gy")
    barrier = pltpu.get_barrier_semaphore()
    for bit in range(bits_of(gx_size)):
        there = mine + (1 << bit) * (1 - 2 * bit_of(mine, bit))
        pl.semaphore_signal(barrier, inc=1, device_id={"gx": there}, device_id_type=pl.DeviceIdType.MESH)
    for away in range(1, gy_size):
        there = (row + away) % gy_size
        pl.semaphore_signal(barrier, inc=1, device_id={"gy": there}, device_id_type=pl.DeviceIdType.MESH)
    pl.semaphore_wait(barrier, bits_of(gx_size) + gy_size - 1)


class Sender:
    def __init__(self, send, recv):
        self.send, self.recv, self.used = send, recv, 0

    def plan(self, src, dst, name, there):
        copy = pltpu.make_async_remote_copy(
            src_ref=src,
            dst_ref=dst,
            send_sem=self.send.at[self.used],
            recv_sem=self.recv.at[self.used],
            device_id={name: there},
            device_id_type=pl.DeviceIdType.MESH,
        )
        self.used += 1
        return copy


def phase(waits=(), act=None, starts=()):
    def run():
        for copy in waits:
            copy.wait()
        if act is not None:
            act()
        for copy in starts:
            copy.start()

    return run


def split_steps(index, size):
    top = bits_of(size) - 1
    core = index % 2
    high, low = bit_of(index, top), bit_of(index, top - 1)
    big, small = 1 << top, 1 << (top - 1)
    first_step = (1 - core) * big * (1 - 2 * high) + core * small * (1 - 2 * low)
    second_step = (1 - core) * small * (1 - 2 * low) + core * big * (1 - 2 * high)
    return core, high, low, first_step, second_step


def gather_column(sender, local, slots, sem, sizes, act=None):
    row = lax.axis_index("gy")
    own = [pltpu.make_async_copy(ref, slot.at[row], sem.at[n]) for n, (ref, slot) in enumerate(zip(local, slots))]
    copies = [
        sender.plan(ref, slot.at[row], "gy", (row + away) % sizes[1])
        for ref, slot in zip(local, slots)
        for away in range(1, sizes[1])
    ]
    return [phase((), None, own + copies), phase(own + copies, act)]


def join_rows(slots, rows_ref, groups):
    gy_size, _, wide = slots.shape
    width = wide // groups
    for i in range(gy_size):
        for k in range(groups):
            low = (k * gy_size + i) * width
            rows_ref[:, low : low + width] = slots[i, :, k * width : (k + 1) * width]


def gather_plane(sender, own, full, sem, sizes):
    gx_size = sizes[0]
    mine = lax.axis_index("gx")
    rows = own.shape[0]
    core, _, _, first_step, second_step = split_steps(mine, gx_size)
    steps = [first_step, second_step]
    for bit in range(1, bits_of(gx_size) - 2)[::-1]:
        steps.append((1 << bit) * (1 - 2 * bit_of(mine, bit)))
    over = 1 - 2 * core

    def view(at):
        return full.at[pl.ds(pl.multiple_of(at * rows, rows), rows), :]

    def push(at, first, there):
        return sender.plan(own if first else view(at), view(at), "gx", there)

    keep = pltpu.make_async_copy(own, view(mine), sem)
    early = [push(mine, True, mine + step) for step in steps]
    over_own = push(mine, True, mine + over)
    shared = [keep, over_own]
    phases = [phase((), None, early + [over_own, keep])]
    held, fresh = [mine], [mine + steps[0]]
    waits = [early[0]]
    for place, step in enumerate(steps[1:], 1):
        held = held + fresh
        copies = [push(at, False, mine + step) for at in held[1:]]
        across = [push(at, False, mine + over) for at in fresh]
        phases.append(phase(waits, None, copies + across))
        shared += across
        waits = [early[place]] + copies
        fresh = [at + step for at in held]
    across = [push(at, False, mine + over) for at in fresh]
    phases.append(phase(waits, None, across))
    phases.append(phase(shared + across))
    return phases


def add_into(target, left, right):
    target[...] = (left[...].astype(jnp.float32) + right[...].astype(jnp.float32)).astype(target.dtype)


def add_arrived(copies, came, kept, out=None):
    def run():
        for k, (copy, view) in enumerate(zip(copies, kept)):
            copy.wait()
            add_into(came.at[k] if out is None else out, came.at[k], view)

    return run


def share_plane(sender, full, halves, out, sizes):
    gx_size = sizes[0]
    mine = lax.axis_index("gx")
    rows = full.shape[0] // gx_size
    core, high, low, first_step, second_step = split_steps(mine, gx_size)

    def block(at):
        return full.at[pl.ds(pl.multiple_of(at * rows, rows), rows), :]

    held, act, phases = block, None, []
    count = gx_size
    for bit in range(bits_of(gx_size)):
        came = halves[bit]
        count //= 2
        own = bit_of(mine, bit)
        if count >= 4:
            step = (1 << bit) * (1 - 2 * own)
            away = [2 * k + 1 - own for k in range(count)]
            kept = [2 * k + own for k in range(count)]
        elif count == 2:
            step = second_step
            away = [(1 - core) * (2 * k + 1 - low) + core * (2 * (1 - high) + k) for k in range(count)]
            kept = [(1 - core) * (2 * k + low) + core * (2 * high + k) for k in range(count)]
        else:
            step = first_step
            last = (1 - core) * high + core * low
            away, kept = [1 - last], [last]
        copies = [sender.plan(held(at), came.at[k], "gx", mine + step) for k, at in enumerate(away)]
        phases.append(phase((), act, copies))
        act = add_arrived(copies, came, [held(at) for at in kept], out if count == 1 else None)
        held = (lambda ref: lambda at: ref.at[at])(came)
    phases.append(phase((), act))
    return phases


def share_column(sender, total, slots, came, out, groups, sizes):
    gy_size = sizes[1]
    row = lax.axis_index("gy")
    width = slots.shape[2] // groups

    def split():
        for i in range(gy_size):
            for k in range(groups):
                low = (k * gy_size + i) * width
                slots[i, :, k * width : (k + 1) * width] = total[:, low : low + width]

    targets = [(row + away) % gy_size for away in range(1, gy_size)]
    copies = [sender.plan(slots.at[there], came.at[n], "gy", there) for n, there in enumerate(targets)]

    def finish():
        total = slots[row].astype(jnp.float32)
        for n, copy in enumerate(copies):
            copy.wait()
            total = total + came[n].astype(jnp.float32)
        out[...] = total

    return [phase((), split, copies), phase((), finish)]


def sum_small(sender, value, came, totals, column, out, sizes):
    held, act, phases = value, None, []
    mine, row = lax.axis_index("gx"), lax.axis_index("gy")
    for bit in range(bits_of(sizes[0])):
        there = mine + (1 << bit) * (1 - 2 * bit_of(mine, bit))
        copy = sender.plan(held, came.at[bit], "gx", there)
        phases.append(phase((), act, [copy]))
        act = add_small(copy, held, came, bit, totals.at[bit])
        held = totals.at[bit]
    copies = [sender.plan(held, column.at[row], "gy", (row + away) % sizes[1]) for away in range(1, sizes[1])]
    phases.append(phase((), act, copies))

    def finish():
        column[row] = held[...]
        for copy in copies:
            copy.wait()
        total = column[0]
        for i in range(1, sizes[1]):
            total = total + column[i]
        out[...] = total

    phases.append(phase((), finish))
    return phases


def add_small(copy, held, came, stage, target):
    def run():
        copy.wait()
        target[...] = held[...] + came[stage]

    return run


def fill_bias(small_all, rel_ref, mask_ref, bias_ref, spread_ref, heads_local):
    gy_size, pad_rows, lanes = small_all.shape
    depth = -(-RELS // 16) * 16
    onehot = (lax.broadcasted_iota(jnp.int32, (depth, SLOT * SLOT), 0) == rel_ref[...]).astype(jnp.bfloat16)
    table = small_all[...].reshape(gy_size * pad_rows, lanes)[:, :depth]
    wide = matmul(table, onehot)
    total = gy_size * pad_rows
    for j in range(SLOT):
        spread_ref[j * total : (j + 1) * total, :] = wide[:, j * SLOT : (j + 1) * SLOT]
    for h in range(gy_size * heads_local):
        line = h // heads_local * pad_rows + 2 + h % heads_local
        one = spread_ref[pl.ds(line, SLOT, stride=total), :]
        low = h % PACK * SLOT
        for w in range(WIN_COUNT):
            bias_ref[w, h // PACK, :, low : low + SLOT] = one + mask_ref[w]


def gather_kernel(sizes, heads_local, qkv_ref, small_ref, proj_ref, fc1_ref, rel_ref, mask_ref,
                  qkv_full, small_all, bias_ref, proj_rows, fc1_rows,
                  qkv_slots, proj_slots, fc1_slots, qkv_rows, spread_ref, send, recv, own_sem, keep_sem):
    greet(*sizes)
    sender = Sender(send, recv)

    def join_later():
        join_rows(proj_slots, proj_rows, 1)
        join_rows(fc1_slots, fc1_rows, 1)

    names = gather_column(sender, [small_ref], [small_all], own_sem.at[0], sizes)
    first = gather_column(sender, [qkv_ref], [qkv_slots], own_sem.at[1], sizes, lambda: join_rows(qkv_slots, qkv_rows, 3))
    second = gather_column(sender, [proj_ref, fc1_ref], [proj_slots, fc1_slots], own_sem.at[2], sizes, join_later)
    plane = gather_plane(sender, qkv_rows, qkv_full, keep_sem.at[0], sizes)
    names[0]()
    first[0]()
    names[1]()
    fill_bias(small_all, rel_ref, mask_ref, bias_ref, spread_ref, heads_local)
    first[1]()
    plane[0]()
    second[0]()
    for run in plane[1:]:
        run()
    second[1]()


def vmem_spec():
    return pl.BlockSpec(memory_space=pltpu.VMEM)


def hbm_spec():
    return pl.BlockSpec(memory_space=pl.ANY)


def in_hbm(value):
    return pltpu.with_memory_space_constraint(value, pltpu.HBM)


def mesh_sizes():
    return lax.axis_size("gx"), lax.axis_size("gy")


def gather_weights(qkv, small, proj_t, fc1, heads_local):
    sizes = mesh_sizes()
    gx_size, gy_size = sizes
    rows = qkv.shape[0]
    _, rel, mask = static_tables(1)
    later = [jax.ShapeDtypeStruct((rows, v.shape[1] * gy_size), v.dtype) for v in (proj_t, fc1)]
    wide = qkv.shape[1] * gy_size
    count = 4 * (gy_size - 1) + gx_size - 1
    bias = (WIN_COUNT, gy_size * heads_local // PACK, SLOT, PACK * SLOT)
    return pl.pallas_call(
        functools.partial(gather_kernel, sizes, heads_local),
        in_specs=[hbm_spec()] * 4 + [vmem_spec()] * 2,
        out_specs=[hbm_spec()] + [vmem_spec()] * 4,
        out_shape=[
            jax.ShapeDtypeStruct((rows * gx_size, wide), qkv.dtype),
            jax.ShapeDtypeStruct((gy_size,) + small.shape, small.dtype),
            jax.ShapeDtypeStruct(bias, jnp.float32),
        ]
        + later,
        scratch_shapes=[pltpu.VMEM((gy_size,) + v.shape, v.dtype) for v in (qkv, proj_t, fc1)]
        + [
            pltpu.VMEM((rows, wide), qkv.dtype),
            pltpu.VMEM((SLOT * gy_size * small.shape[0], SLOT), jnp.float32),
            pltpu.SemaphoreType.DMA((count,)), pltpu.SemaphoreType.DMA((count,)), pltpu.SemaphoreType.DMA((3, 2)),
            pltpu.SemaphoreType.DMA((1,)),
        ],
        compiler_params=pltpu.CompilerParams(collective_id=0, has_side_effects=True, vmem_limit_bytes=14 << 20),
        name="gather_weights",
    )(qkv, small, in_hbm(proj_t), in_hbm(fc1), in_hbm(jnp.asarray(rel.reshape(1, -1))), in_hbm(jnp.asarray(mask)))


def table_gradient(d_bias_ref, rel_ref, spread_ref, table_ref):
    groups = d_bias_ref.shape[0]
    heads, depth = groups * PACK, table_ref.shape[1]
    for h in range(heads):
        low = h % PACK * SLOT
        spread_ref[pl.ds(h, SLOT, stride=heads), :] = d_bias_ref[h // PACK, :, low : low + SLOT]
    total = jnp.zeros((heads, depth), jnp.float32)
    step = 8
    for at in range(0, SLOT, step):
        pairs = jnp.concatenate([spread_ref[j * heads : (j + 1) * heads, :] for j in range(at, at + step)], 1)
        spots = lax.broadcasted_iota(jnp.int32, (depth, step * SLOT), 0)
        onehot = (spots == rel_ref[:, at * SLOT : (at + step) * SLOT]).astype(jnp.bfloat16)
        for _ in range(3):
            high = pairs.astype(jnp.bfloat16)
            total = total + matmul_nt(high, onehot)
            pairs = pairs - high.astype(jnp.float32)
    table_ref[...] = total


def share_kernel(sizes, groups, whole_count, *refs):
    gx_bits = bits_of(sizes[0])
    arrays = len(groups)
    refs = list(refs)

    def take(count):
        out = refs[:count]
        del refs[:count]
        return out

    inputs, (small,) = take(arrays), take(1)
    act, fc2_full, resid, shift, d_bias, rel = take(6)
    outs, (small_out, output, table_out) = take(arrays), take(3)
    planes = [take(gx_bits) for _ in range(whole_count)]
    totals, slots, columns = take(whole_count), take(arrays), take(arrays)
    small_came, small_totals, small_column, table_came, table_totals, table_column, table, spread_ref, send, recv = take(10)
    greet(*sizes)
    sender = Sender(send, recv)
    streams = []
    for n in range(arrays):
        phases = share_plane(sender, inputs[n], planes[n], totals[n], sizes) if n < whole_count else []
        total = totals[n] if n < whole_count else inputs[n]
        column = share_column(sender, total, slots[n], columns[n], outs[n], groups[n], sizes)
        if phases:
            last, after = phases.pop(), column.pop(0)
            phases.append(both(last, after))
        streams.append(phases + column)
    streams.append(sum_small(sender, small, small_came, small_totals, small_column, small_out, sizes))
    late = sum_small(sender, table, table_came, table_totals, table_column, table_out, sizes)
    late[0] = both(lambda: table_gradient(d_bias, rel, spread_ref, table), late[0])
    streams.append(late)
    width = output.shape[1]
    chunk = min(2 * 128, width)
    rest = list(range(0, width, chunk))
    place = 0
    while any(streams):
        for queue in streams:
            if queue:
                queue.pop(0)()
        place += 1
        if place >= 2 and rest:
            low = rest.pop(0)
            cols = slice(low, low + chunk)
            output[:, cols] = (resid[:, cols] + matmul_nt(act[...], fc2_full[cols, :]) + shift[:, cols]).astype(output.dtype)
    for low in rest:
        cols = slice(low, low + chunk)
        output[:, cols] = (resid[:, cols] + matmul_nt(act[...], fc2_full[cols, :]) + shift[:, cols]).astype(output.dtype)


def both(one, other):
    def run():
        one()
        other()

    return run


def share_sums(fulls, rows_sums, groups, small, product, d_bias):
    sizes = mesh_sizes()
    gx_size, gy_size = sizes
    gx_bits = bits_of(gx_size)
    rows = fulls[0].shape[0] // gx_size
    arrays = tuple(fulls) + tuple(rows_sums)
    planes, slots, columns = [], [], []
    for full in fulls:
        planes += [pltpu.VMEM((gx_size >> (bit + 1), rows, full.shape[1]), full.dtype) for bit in range(gx_bits)]
    for value in arrays:
        wide = value.shape[1] // gy_size
        slots.append(pltpu.VMEM((gy_size, rows, wide), value.dtype))
        columns.append(pltpu.VMEM((gy_size - 1, rows, wide), value.dtype))
    count = len(fulls) * (gx_size - 1) + len(arrays) * (gy_size - 1) + 2 * (gx_bits + gy_size - 1)
    heads, depth = d_bias.shape[0] * PACK, -(-RELS // 128) * 128
    _, rel, _ = static_tables(1)
    return pl.pallas_call(
        functools.partial(share_kernel, sizes, groups, len(fulls)),
        in_specs=[vmem_spec()] * (len(arrays) + 7),
        out_specs=[vmem_spec()] * (len(arrays) + 3),
        out_shape=[jax.ShapeDtypeStruct((rows, value.shape[1] // gy_size), jnp.float32) for value in arrays]
        + [jax.ShapeDtypeStruct(small.shape, small.dtype), jax.ShapeDtypeStruct(product[2].shape, jnp.bfloat16), jax.ShapeDtypeStruct((heads, depth), jnp.float32)],
        scratch_shapes=planes + [pltpu.VMEM((rows, full.shape[1]), full.dtype) for full in fulls] + slots + columns + [
            pltpu.VMEM((gx_bits,) + small.shape, small.dtype),
            pltpu.VMEM((gx_bits,) + small.shape, small.dtype),
            pltpu.VMEM((gy_size,) + small.shape, small.dtype),
            pltpu.VMEM((gx_bits, heads, depth), jnp.float32),
            pltpu.VMEM((gx_bits, heads, depth), jnp.float32),
            pltpu.VMEM((gy_size, heads, depth), jnp.float32),
            pltpu.VMEM((heads, depth), jnp.float32),
            pltpu.VMEM((SLOT * heads, SLOT), jnp.float32),
            pltpu.SemaphoreType.DMA((count,)),
            pltpu.SemaphoreType.DMA((count,)),
        ],
        compiler_params=pltpu.CompilerParams(collective_id=1, has_side_effects=True, vmem_limit_bytes=18 << 20),
        name="share_sums",
    )(*arrays, small, *product, d_bias, jnp.asarray(rel.reshape(1, -1)))


def forward_stage(
    sizes, qkv_ref, perm_ref, perm_t_ref, bias_ref, owner_ref, proj_rows, fc1_rows, fc2_local,
    context_ref, windows_ref, probs_ref, proj_full, fc1_full, fc2_full,
    ctx_ref, fc2_slots, fc2_rows, send, recv, keep_sem, own_sem,
):
    image, last = pl.program_id(0), pl.num_programs(0) - 1

    @pl.when(image == 0)
    def _():
        greet(*sizes)

    sender = Sender(send, recv)
    own = (proj_rows, fc1_rows, fc2_rows)
    fulls = (proj_full, fc1_full, fc2_full)
    streams = [gather_plane(sender, own[n], fulls[n], keep_sem.at[n], sizes) for n in range(3)]
    column = gather_column(sender, [fc2_local], [fc2_slots], own_sem, sizes, lambda: join_rows(fc2_slots, fc2_rows, 1))

    @pl.when(image == 0)
    def _():
        column[0]()
        streams[0][0]()
        streams[1][0]()

    @pl.when(image == jnp.minimum(2, last))
    def _():
        streams[0][1]()
        column[1]()
        streams[2][0]()

    @pl.when(image == last)
    def _():
        streams[1][1]()

    forward_kernel(
        qkv_ref, perm_ref, perm_t_ref, bias_ref, owner_ref, context_ref, windows_ref, probs_ref, ctx_ref
    )

    @pl.when(image == last)
    def _():
        streams[2][1]()
        for place in range(2, len(streams[0])):
            for phases in streams:
                phases[place]()


def backward_stage(
    sizes, d_context_ref, windows_ref, probs_ref, perm_ref, perm_t_ref, owner_ref, d_fc1_ref, d_fc2_ref,
    d_mixed_ref, d_bias_ref, d_qv_ref, fc1_sum, fc2_sum, d_ctx_ref, d_win_ref, *rest,
):
    image, last = pl.program_id(0), pl.num_programs(0) - 1
    gx_bits = bits_of(sizes[0])
    fc1_halves, fc2_halves, (send, recv) = rest[:gx_bits], rest[gx_bits : 2 * gx_bits], rest[2 * gx_bits :]

    @pl.when(image == 0)
    def _():
        greet(*sizes)

    sender = Sender(send, recv)
    streams = [
        share_plane(sender, d_fc1_ref, fc1_halves, fc1_sum, sizes),
        share_plane(sender, d_fc2_ref, fc2_halves, fc2_sum, sizes),
    ]

    @pl.when(image == 0)
    def _():
        for phases in streams:
            phases[0]()

    def between(slot):
        for when, n, place in ((1, 0, 1), (2, 1, 1), (5, 0, 2), (7, 1, 2)):
            @pl.when(slot == jnp.minimum(when, 2 * last + when % 2))
            def _(phases=streams[n], place=place):
                phases[place]()

    backward_kernel(
        d_context_ref, windows_ref, probs_ref, perm_ref, perm_t_ref, owner_ref,
        d_mixed_ref, d_bias_ref, d_qv_ref, d_ctx_ref, d_win_ref, between,
    )

    @pl.when(image == last)
    def _():
        for place in range(3, len(streams[0])):
            for phases in streams:
                phases[place]()


def pack_rows(values):
    rows = []
    for value in values:
        flat = value.reshape(-1)
        rows.append(jnp.pad(flat, (0, -flat.shape[0] % 1024)).reshape(-1, 128))
    return jnp.concatenate(rows, 0)


def unpack_rows(packed, shapes):
    at, out = 0, []
    for shape in shapes:
        size = int(np.prod(shape))
        count = (size + 1023) // 1024 * 8
        out.append(packed[at : at + count].reshape(-1)[:size].reshape(shape))
        at += count
    return out


def own_columns(summed, axis):
    size = summed.shape[axis] // lax.axis_size("gy")
    return lax.dynamic_slice_in_dim(summed, lax.axis_index("gy") * size, size, axis)


def local_live(tok_local, live_images):
    position = lax.axis_index("gy")
    per_device = tok_local // (GRID * GRID)
    slot_index = position * per_device + jnp.arange(tok_local, dtype=jnp.int32) // (GRID * GRID)
    return slot_index < live_images[0]


def blocked_layer(block_input, cotangent, live_images, params):
    (
        ln1_gain,
        ln1_bias,
        qkv_weight,
        qv_bias,
        rel_table,
        proj_weight,
        proj_bias,
        ln2_gain,
        ln2_bias,
        fc1_weight,
        fc1_bias,
        fc2_weight,
        fc2_bias,
    ) = params
    tok_local, width = block_input.shape
    block_rows = qkv_weight.shape[0]
    part, hidden_local = qkv_weight.shape[2], fc1_weight.shape[1]
    heads_local = rel_table.shape[1]

    def lane_row(value):
        value = value.reshape(value.shape[0], -1)
        return jnp.pad(value, ((0, 0), (0, hidden_local - value.shape[1])))

    small = jnp.concatenate([fc1_bias[None], lane_row(qv_bias.reshape(1, -1)), lane_row(rel_table.T)], 0)
    small = jnp.pad(small, ((0, ROW_PAD - small.shape[0]), (0, 0)))
    qkv_flat, small, bias, *later = gather_weights(
        qkv_weight.reshape(block_rows, -1), small, proj_weight.T, fc1_weight, heads_local
    )
    later.append(fc2_weight.T)
    fc1_bias = small[:, 0].reshape(-1)
    qv_bias = small[:, 1, : 2 * part].reshape(-1, 2, part).transpose(1, 0, 2).reshape(2, -1)
    gain_one = ln1_gain.astype(jnp.float32)
    gain_two = ln2_gain.astype(jnp.float32)
    resid = block_input.astype(jnp.float32)
    normed_one, scale_one, pre_one = layer_norm(resid, gain_one, ln1_bias.astype(jnp.float32))
    hidden_one = (pre_one.astype(jnp.bfloat16))
    bias_row = jnp.stack([qv_bias[0], jnp.zeros_like(qv_bias[0]), qv_bias[1]]).reshape(1, 3 * width)
    mixed = (matmul(hidden_one, qkv_flat) + bias_row.astype(jnp.float32)).astype(jnp.bfloat16)
    tables = attention_tables(tok_local // IMAGE)
    context, windows, probs, proj_cols, fc1_rows, fc2_cols = attend_forward(mixed, tables, bias, later)
    resid_one = resid + (matmul_nt(context, proj_cols)) + proj_bias.astype(jnp.float32)
    normed_two, scale_two, pre_two = layer_norm(resid_one, gain_two, ln2_bias.astype(jnp.float32))
    hidden_two = (pre_two.astype(jnp.bfloat16))
    pre_act = matmul(hidden_two, fc1_rows) + fc1_bias.astype(jnp.float32)
    act_full, slope = gelu_parts(pre_act)
    act_low, slope = lax.optimization_barrier((act_full.astype(jnp.bfloat16), slope.astype(jnp.bfloat16)))
    live_rows = local_live(tok_local, live_images)
    grad_out = jnp.where(live_rows[:, None], cotangent, jnp.zeros_like(cotangent))
    grad_float = grad_out.astype(jnp.float32)
    grad_full = (grad_out)
    d_fc2_bias = jnp.sum(grad_float, 0)
    d_fc2_weight = matmul_tn(grad_full, act_low).astype(jnp.bfloat16)
    d_pre = matmul(grad_full, fc2_cols) * slope
    d_fc1_bias = jnp.sum(d_pre, 0)
    d_pre_low = d_pre.astype(jnp.bfloat16)
    d_fc1_weight = matmul_tn(hidden_two, d_pre_low).astype(jnp.bfloat16)
    d_hidden_two = (matmul_nt(d_pre_low, fc1_rows))
    d_ln2_gain = jnp.sum(d_hidden_two * normed_two, 0)
    d_ln2_bias = jnp.sum(d_hidden_two, 0)
    d_resid_one = grad_float + norm_back(d_hidden_two, normed_two, scale_two, gain_two)
    d_proj_bias = jnp.sum(d_resid_one, 0)
    d_resid_full = (d_resid_one.astype(jnp.bfloat16))
    d_proj_weight = matmul_tn(d_resid_full, context).astype(jnp.bfloat16)
    d_context = matmul(d_resid_full, proj_cols).astype(jnp.bfloat16)
    d_mixed, d_qv_bias, d_bias, sums = attend_backward(d_context, windows, probs, tables, (d_fc1_weight, d_fc2_weight))
    d_qkv_weight = matmul_tn(hidden_one, d_mixed).astype(jnp.bfloat16)
    d_hidden_one = (matmul_nt(d_mixed, qkv_flat))
    d_ln1_gain = jnp.sum(d_hidden_one * normed_one, 0)
    d_ln1_bias = jnp.sum(d_hidden_one, 0)
    d_input = (d_resid_one + norm_back(d_hidden_one, normed_one, scale_one, gain_one)).astype(
        jnp.bfloat16
    )
    own = (d_ln1_gain, d_ln1_bias, d_proj_bias, d_ln2_gain, d_ln2_bias, d_fc2_bias, d_qv_bias, d_fc1_bias)
    product = (act_low, fc2_cols, resid_one, fc2_bias.astype(jnp.float32)[None])
    d_qkv_weight, d_proj_weight, d_fc1_weight, d_fc2_weight, sums, output, d_table = share_sums(
        (d_qkv_weight, d_proj_weight), sums, (3, 1, 1, 1), pack_rows(own), product, d_bias
    )
    d_fc2_weight = d_fc2_weight.T
    d_proj_weight = d_proj_weight.T
    d_qkv_weight = d_qkv_weight.reshape(block_rows, 3, part)
    sums = unpack_rows(sums, [value.shape for value in own])
    norm_sums = sums[:6]
    head_sums = (own_columns(sums[6], 1), own_columns(d_table, 0)[:, :RELS].T, own_columns(sums[7], 0))
    return (
        output,
        d_input,
        norm_sums[0],
        norm_sums[1],
        d_qkv_weight,
        head_sums[0],
        head_sums[1],
        d_proj_weight,
        norm_sums[2],
        norm_sums[3],
        norm_sums[4],
        d_fc1_weight,
        head_sums[2],
        d_fc2_weight,
        norm_sums[5],
    )


def shards(
    block_input,
    cotangent,
    live_images,
    ln1_gain,
    ln1_bias,
    qkv_weight,
    qv_bias,
    rel_table,
    proj_weight,
    proj_bias,
    ln2_gain,
    ln2_bias,
    fc1_weight,
    fc1_bias,
    fc2_weight,
    fc2_bias,
):
    params = (
        ln1_gain,
        ln1_bias,
        qkv_weight,
        qv_bias,
        rel_table,
        proj_weight,
        proj_bias,
        ln2_gain,
        ln2_bias,
        fc1_weight,
        fc1_bias,
        fc2_weight,
        fc2_bias,
    )
    return blocked_layer(block_input, cotangent, live_images, params)


def solution(mesh):
    return jax.shard_map(
        shards,
        mesh=mesh,
        in_specs=(
            P(("gx", "gy"), None),
            P(("gx", "gy"), None),
            P("gx"),
            P(),
            P(),
            P("gx", None, "gy"),
            P(None, "gy"),
            P(None, "gy"),
            P("gy", "gx"),
            P(),
            P(),
            P(),
            P("gx", "gy"),
            P("gy"),
            P("gy", "gx"),
            P(),
        ),
        out_specs=(
            P(("gx", "gy"), None),
            P(("gx", "gy"), None),
            P(),
            P(),
            P("gx", None, "gy"),
            P(None, "gy"),
            P(None, "gy"),
            P("gy", "gx"),
            P(),
            P(),
            P(),
            P("gx", "gy"),
            P("gy"),
            P("gy", "gx"),
            P(),
        ),
        check_vma=False,
    )
```
